32 devices in a mesh: row: 4 (over z), col: 2 (over x), depth: 4 (over y, core).
Axes of the slice: x: 2, y: 2, z: 4, core: 2. Of those that a mesh axis runs over, the one named last changes fastest.
Arguments:
- tokens: bfloat16 [2560, 8192], P(('row', 'depth'), 'col'), may hold values from -6 to 6
- weight: bfloat16 [8192, 4096], P('row', 'col'), may hold values from -0.0625 to 0.0625
- cotangent: bfloat16 [2560, 4096], P(('row', 'depth'), 'col'), may hold values from -6 to 6
- master: float32 [8192, 4096], P(('row', 'depth'), 'col'), may hold values from -0.1 to 0.1
- first_moment: float32 [8192, 4096], P(('row', 'depth'), 'col'), may hold values from -6 to 6
- second_moment: float32 [8192, 4096], P(('row', 'depth'), 'col'), may hold values from 0.1 to 10
Outputs:
- queries: bfloat16 [2560, 4096], P(('row', 'depth'), 'col')
- token_grad: bfloat16 [2560, 8192], P(('row', 'depth'), 'col')
- new_master: float32 [8192, 4096], P(('row', 'depth'), 'col')
- new_first: float32 [8192, 4096], P(('row', 'depth'), 'col')
- new_second: float32 [8192, 4096], P(('row', 'depth'), 'col')
- new_weight: bfloat16 [8192, 4096], P('row', 'col')
The draws below stay inside these ranges and needn't reach their ends.
All inputs are finite; a program needn't handle non-finite values.
Results may differ from the reference program's by a relative error of at most 0.001.
Values may be sent and summed in bfloat16 or wider, within the bound.
A program may use at most 128 MiB of HBM per device.

```python
import math
import jax
import jax.numpy as jnp

D = 8192
HQ = 4096
TOKENS = 2560


def strengthened(values, rng, source, target, blocks, factor):
    owner, partner = [(jnp.arange(values.shape[axis_at]) // (values.shape[axis_at] // blocks)).reshape([-1 if axis == axis_at else 1 for axis in range(values.ndim)]) for axis_at in (source, target)]
    chosen = jax.random.permutation(rng, blocks)[partner]
    strong = (owner == chosen) | (owner == (partner + blocks // 2) % blocks)
    return jnp.where(strong, factor * values, values)


def shard_levels(rng, dims, split, smallest, largest):
    def one(dim, blocks):
        heights = jax.random.uniform(jax.random.fold_in(jax.random.fold_in(rng, 6), dim), (blocks,), jnp.float32, smallest / len(split), largest / len(split))
        return jnp.repeat(jnp.exp(heights), dims[dim] // blocks).reshape((-1,) + (1,) * (len(dims) - dim - 1))

    gain = one(*split[0])
    for cut in split[1:]:
        gain = gain * one(*cut)
    return gain


def bell_draw(stream_key, dims, width, bound, shards=(), held_as=jnp.bfloat16):
    drawn = width * jax.random.normal(stream_key, dims, jnp.float32)
    if shards:
        drawn = drawn * shard_levels(stream_key, dims, shards, -0.22, 0.18)
    return jnp.clip(drawn, -bound, bound).astype(held_as)


def noise_with(key, shape, scale, reach, cuts, heavy, dtype=jnp.bfloat16):
    values = scale * jax.random.normal(key, shape, jnp.float32)
    if cuts:
        values = values * shard_levels(key, shape, cuts, -0.22, 0.18)
    return jnp.clip(strengthened(values, jax.random.fold_in(key, 3), *heavy), -reach, reach).astype(dtype)


def setup_inputs(seed: int = 0) -> dict:
    arg_keys = jax.random.split(jax.random.key(seed), 7)
    return {
        "tokens": noise_with(arg_keys[0], (TOKENS, D), 1.0, 6.0, ((0, 16), (1, 2)), (0, 1, 16, 2.0)),
        "weight": bell_draw(arg_keys[1], (D, HQ), D ** -0.5, 0.0625, ((0, 4), (1, 2))),
        "cotangent": bell_draw(arg_keys[2], (TOKENS, HQ), 1.0, 6.0, ((0, 16), (1, 2))),
        "master": jnp.clip(jax.random.uniform(arg_keys[3], (D, HQ), jnp.float32, -0.1, 0.1) * shard_levels(arg_keys[3], (D, HQ), ((0, 16), (1, 2)), -0.4, 0.0), -0.1, 0.1),
        "first_moment": bell_draw(arg_keys[4], (D, HQ), 1.0, 6.0, ((0, 16), (1, 2)), jnp.float32),
        "second_moment": jnp.clip(jnp.exp(math.log(10.0) - 4.6051702 * jax.random.uniform(arg_keys[5], (D, HQ), jnp.float32) ** shard_levels(arg_keys[5], (D, HQ), ((0, 16), (1, 2)), -0.2, 0.2)), 0.1, 10.0),
    }


beta_one = 0.9
beta_two = 0.95
learn_rate = 0.02
decay_rate = 0.1
adam_eps = 1e-08
bias_one = 1.0 - 0.9 ** 50
bias_two = 1.0 - 0.95 ** 50

def reference(tokens, weight, cotangent, master, first_moment, second_moment):
    queries = jnp.dot(tokens, weight, preferred_element_type=jnp.float32).astype(jnp.bfloat16)
    token_grad = jnp.dot(cotangent, weight.T, preferred_element_type=jnp.float32).astype(jnp.bfloat16)
    grad = jnp.dot(tokens.T, cotangent, preferred_element_type=jnp.float32) * (1.0 / math.sqrt(TOKENS))
    new_first = beta_one * first_moment + (1.0 - beta_one) * grad
    new_second = beta_two * second_moment + (1.0 - beta_two) * grad * grad
    step_value = new_first / bias_one / (jnp.sqrt(new_second / bias_two) + adam_eps)
    new_master = master - learn_rate * (step_value + decay_rate * master)
    new_weight = new_master.astype(jnp.bfloat16)
    return (queries, token_grad, new_master, new_first, new_second, new_weight)
```

```python
import functools
import itertools
import math

import jax
import jax.numpy as jnp
from jax import lax
from jax.experimental import pallas as pl
from jax.experimental.pallas import tpu as pltpu
from jax.sharding import PartitionSpec as P

beta_one = 0.9
beta_two = 0.95
learn_rate = 0.02
decay_rate = 0.1
adam_eps = 1e-08
bias_one = 1.0 - 0.9**50
bias_two = 1.0 - 0.95**50


def swap(value, axis, step):
    size = lax.axis_size(axis)
    return lax.ppermute(value, axis, [(i, i ^ step) for i in range(size)])


def spread(value, axis):
    pieces = [value]
    for step in range(1, lax.axis_size(axis)):
        top = 1 << (step.bit_length() - 1)
        low = step & -step
        pieces.append(swap(pieces[step - low], axis, low) if step != top else swap(value, axis, step))
    return pieces


def in_order(pieces, axis, dim):
    me = lax.axis_index(axis)
    size = pieces[0].shape[dim]
    shape = list(pieces[0].shape)
    shape[dim] = size * len(pieces)
    whole = jnp.zeros(shape, pieces[0].dtype)
    for step, piece in enumerate(pieces):
        whole = lax.dynamic_update_slice_in_dim(whole, piece, (me ^ step) * size, dim)
    return whole


def plain(tokens, weight, cotangent, master, first_moment, second_moment):
    rows, cols, depths = lax.axis_size("row"), lax.axis_size("col"), lax.axis_size("depth")
    col_at, depth_at = lax.axis_index("col"), lax.axis_index("depth")
    block = tokens.shape[0]
    total_tokens = block * rows * depths
    grad_scale = 1.0 / math.sqrt(total_tokens)
    full_rows = in_order(spread(tokens, "col"), "col", 1)
    line_cotangent = lax.all_gather(cotangent, "row", axis=0, tiled=True)
    line_tokens = lax.all_to_all(full_rows, "row", split_axis=1, concat_axis=0, tiled=True)
    features = weight.shape[0] // cols
    parts = []
    for step in reversed(range(cols)):
        panel = lax.dynamic_slice_in_dim(weight, (col_at ^ step) * features, features, 0)
        part = lax.dot_general(
            line_cotangent, panel, (((1,), (1,)), ((), ())), preferred_element_type=jnp.float32
        )
        parts.append(swap(part, "col", step) if step else part)
    piece = sum(parts[1:], parts[0]).astype(jnp.bfloat16)
    partial_queries = jnp.dot(line_tokens, weight, preferred_element_type=jnp.float32)
    queries = lax.psum_scatter(partial_queries, "row", scatter_dimension=0, tiled=True).astype(
        jnp.bfloat16
    )
    piece = lax.all_to_all(
        piece.reshape(rows, block, -1), "row", split_axis=0, concat_axis=0, tiled=True
    )
    piece = lax.all_to_all(
        piece.reshape(cols, rows // cols, block, -1), "col", split_axis=0, concat_axis=0, tiled=True
    )
    token_grad = piece.transpose(2, 1, 0, 3).reshape(tokens.shape)
    shard = line_tokens.shape[1] // depths
    product = 0.0
    for step, other_cotangent in enumerate(spread(line_cotangent, "depth")):
        slab = lax.dynamic_slice_in_dim(line_tokens, (depth_at ^ step) * shard, shard, 1)
        slab = swap(slab, "depth", step) if step else slab
        product = product + lax.dot_general(
            slab, other_cotangent, (((0,), (0,)), ((), ())), preferred_element_type=jnp.float32
        )
    grad = product * grad_scale
    new_first = beta_one * first_moment + (1.0 - beta_one) * grad
    new_second = beta_two * second_moment + (1.0 - beta_two) * grad * grad
    step_value = new_first / bias_one / (jnp.sqrt(new_second / bias_two) + adam_eps)
    new_master = master - learn_rate * (step_value + decay_rate * master)
    shard_weight = new_master.astype(jnp.bfloat16)
    new_weight = in_order(spread(shard_weight, "depth"), "depth", 0)
    return (queries, token_grad, new_master, new_first, new_second, new_weight)


MESH = pl.DeviceIdType.MESH
WIDE = 512
STATE_PARTS = 8
SEND_PARTS = 4


def flip(index, step):
    for bit in range(step.bit_length()):
        if step >> bit & 1:
            index = index + (1 << bit) - 2 * (1 << bit) * (index // (1 << bit) % 2)
    return index


def relay_of(step):
    low = step & -step
    return step - low, low


def fused(
    rows,
    depths,
    grad_scale,
    tokens_hbm,
    weight_hbm,
    cotangent_hbm,
    master_hbm,
    first_hbm,
    second_hbm,
    queries_out,
    token_grad_out,
    master_out,
    first_out,
    second_out,
    weight_out,
    weight,
    early,
    line,
    cots,
    slabs,
    turned,
    partial,
    running,
    split,
    inbound,
    piece,
    landed,
    product,
    shard,
    relayed,
    query,
    states,
    results,
    local_sem,
    send_sem,
    recv_sem,
):
    row, col, depth = lax.axis_index("row"), lax.axis_index("col"), lax.axis_index("depth")
    other = 1 - col
    block, width = line.shape[1], line.shape[2]
    half = block // 2
    features = width // 2
    out_width = weight.shape[1]
    owned = shard.shape[0]
    per_col = rows // 2
    singles = [1 << bit for bit in range(depths.bit_length() - 1)]
    composites = [step for step in range(1, depths) if step & (step - 1)]
    stored = sorted({relay_of(step)[0] for step in composites})

    sends = itertools.count()
    locals_ = itertools.count()
    places = itertools.count()
    pending = []

    def slots(count):
        return [next(places) for _ in range(count)][0]

    at_early = slots(1)
    at_line = slots(rows)
    at_cross = slots(rows)
    at_cot = slots(rows)
    at_spread = slots(depths * rows)
    at_part = slots(rows)
    at_piece = slots(rows)
    at_final = slots(rows)
    at_run = slots(rows + 1)
    at_slab = slots(depths)
    at_weight = slots(depths * SEND_PARTS)

    def where(cond, act):
        if cond is None:
            act()
        else:
            pl.when(cond)(act)

    def both(one, two):
        return two if one is None else jnp.logical_and(one, two)

    def go(cond, source, target, place, row_to=None, col_to=None, depth_to=None):
        peer = (
            row if row_to is None else row_to,
            col if col_to is None else col_to,
            depth if depth_to is None else depth_to,
        )
        copy = pltpu.make_async_remote_copy(
            src_ref=source,
            dst_ref=target,
            send_sem=send_sem.at[next(sends)],
            recv_sem=recv_sem.at[place],
            device_id=peer,
            device_id_type=MESH,
        )
        where(cond, copy.start)
        pending.append((cond, copy.wait_send))

    def arrived(cond, target, place):
        copy = pltpu.make_async_remote_copy(
            src_ref=target,
            dst_ref=target,
            send_sem=send_sem.at[0],
            recv_sem=recv_sem.at[place],
            device_id=(row, other, depth),
            device_id_type=MESH,
        )
        where(cond, copy.wait_recv)

    def load(cond, source, target):
        copy = pltpu.make_async_copy(source, target, local_sem.at[next(locals_)])
        where(cond, copy.start)
        return cond, copy.wait

    barrier = pltpu.get_barrier_semaphore()
    peers = [((row + step) % rows, col, depth) for step in range(1, rows)]
    peers += [(row, other, depth)]
    peers += [(row, col, flip(depth, step)) for step in range(1, depths)]
    for peer in peers:
        pl.semaphore_signal(barrier, inc=1, device_id=peer, device_id_type=MESH)
    pl.semaphore_wait(barrier, len(peers))

    mine = pl.ds(pl.multiple_of(col * half, half), half)
    theirs = pl.ds(pl.multiple_of(other * half, half), half)
    owner = row // per_col

    def features_of(at):
        return pl.ds(pl.multiple_of(at % per_col * width, width), width)

    go(None, tokens_hbm.at[theirs], early, at_early, col_to=other)
    for step in reversed(range(1, rows)):
        there = (row + step) % rows
        go(
            there // per_col == col,
            tokens_hbm.at[mine, features_of(there)],
            line.at[row, mine],
            at_line + row,
            row_to=there,
        )
    right, left = row + 1 < rows, row >= 1
    go(right, cotangent_hbm, cots.at[0, row], at_cot + row, row_to=row + 1)
    go(left, cotangent_hbm, cots.at[0, row], at_cot + row, row_to=row - 1)
    for step in reversed(singles):
        go(
            None,
            cotangent_hbm,
            cots.at[step, row],
            at_spread + step * rows + row,
            depth_to=flip(depth, step),
        )
    weight_here = load(None, weight_hbm, weight)
    cot_here = load(None, cotangent_hbm, cots.at[0, row])
    own_tokens = [
        load(owner == col, tokens_hbm.at[mine, features_of(row)], line.at[row, mine])
    ]
    go(
        owner == col,
        tokens_hbm.at[mine, features_of(row)],
        line.at[row, mine],
        at_cross + row,
        col_to=other,
    )
    state_refs = (master_hbm, first_hbm, second_hbm)
    result_refs = (master_out, first_out, second_out)
    part_rows = owned // STATE_PARTS
    state_sems = [[next(locals_) for _ in range(3)] for _ in range(2)]
    result_sems = [[next(locals_) for _ in range(3)] for _ in range(2)]

    def state_copies(part):
        return [
            pltpu.make_async_copy(
                ref.at[pl.ds(part * part_rows, part_rows)],
                states.at[part % 2, i],
                local_sem.at[state_sems[part % 2][i]],
            )
            for i, ref in enumerate(state_refs)
        ]

    def result_copies(part):
        return [
            pltpu.make_async_copy(
                results.at[part % 2, i],
                ref.at[pl.ds(part * part_rows, part_rows)],
                local_sem.at[result_sems[part % 2][i]],
            )
            for i, ref in enumerate(result_refs)
        ]

    for part in range(2):
        for copy in state_copies(part):
            copy.start()

    arrived(None, early, at_early)
    for step in reversed(range(1, rows)):
        there = (row + step) % rows
        go(
            there // per_col != col,
            early.at[:, features_of(there)],
            line.at[row, mine],
            at_line + row,
            row_to=there,
        )
    own_tokens.append(load(owner != col, early.at[:, features_of(row)], line.at[row, mine]))
    go(
        owner != col,
        early.at[:, features_of(row)],
        line.at[row, mine],
        at_cross + row,
        col_to=other,
    )

    tiles = width // min(WIDE, features)
    tile = width // tiles

    def gradient_part(at):
        def tile_of(index, carry):
            start = pl.multiple_of(index * tile, tile)
            side = start // features
            value = lax.dot_general(
                cots[0, at],
                weight[pl.ds(start, tile)],
                (((1,), (1,)), ((), ())),
                preferred_element_type=jnp.float32,
            )
            inside = pl.ds(pl.multiple_of(start % features, tile), tile)
            split[side, at, :, inside] = value
            return carry

        lax.fori_loop(0, tiles, tile_of, 0)

    def send_part(cond, at):
        go(cond, split.at[other, at], inbound.at[at], at_part + at, col_to=other)

    weight_here[1]()
    cot_here[1]()
    gradient_part(row)
    send_part(None, row)

    def spread_on(step_from_row, cond, at):
        for step in composites:
            have, low = relay_of(step)
            arrived(cond, cots.at[have, at], at_spread + have * rows + at)
            go(
                cond,
                cots.at[have, at],
                cots.at[step, at],
                at_spread + step * rows + at,
                depth_to=flip(depth, low),
            )

    for step in range(1, rows):
        sides = [(row - step, row >= step, row + 1 < rows, row + 1)]
        sides += [(row + step, row + step < rows, row >= 1, row - 1)]
        for at, cond, relay, there in sides:
            arrived(cond, cots.at[0, at], at_cot + at)
            go(both(cond, relay), cots.at[0, at], cots.at[0, at], at_cot + at, row_to=there)
            for single in reversed(singles):
                go(
                    cond,
                    cots.at[0, at],
                    cots.at[single, at],
                    at_spread + single * rows + at,
                    depth_to=flip(depth, single),
                )
        for at, cond, _, _ in sides:
            arrived(cond, line.at[at, mine], at_line + at)
            go(cond, line.at[at, mine], line.at[at, mine], at_cross + at, col_to=other)
        if step == 1:
            spread_on(0, None, row)
        else:
            spread_on(step - 1, row >= step - 1, row - step + 1)
            spread_on(step - 1, row + step - 1 < rows, row + step - 1)

        def one_side(index, carry, step=step):
            at = row + step * (2 * index - 1)

            @pl.when(jnp.logical_and(at >= 0, at < rows))
            def _():
                gradient_part(at)

            return carry

        lax.fori_loop(0, 2, one_side, 0)
        for at, cond, _, _ in sides:
            send_part(cond, at)
    spread_on(rows - 1, row >= rows - 1, row - rows + 1)
    spread_on(rows - 1, row + rows - 1 < rows, row + rows - 1)

    for cond, wait in own_tokens:
        where(cond, wait)
    for at in range(rows):
        arrived(None, line.at[at, theirs], at_cross + at)
    for step in reversed(range(1, depths)):
        there = flip(depth, step)
        go(
            None,
            line.at[:, :, pl.ds(pl.multiple_of(there * owned, owned), owned)],
            slabs.at[step - 1],
            at_slab + step,
            depth_to=there,
        )

    query_tiles = out_width // min(WIDE, out_width)
    query_tile = out_width // query_tiles

    def query_part(at):
        def tile_of(index, carry):
            across = pl.ds(pl.multiple_of(index * query_tile, query_tile), query_tile)
            partial[at, :, across] = jnp.dot(
                line[at], weight[:, across], preferred_element_type=jnp.float32
            )
            return carry

        lax.fori_loop(0, query_tiles, tile_of, 0)

    def run_right(cond, at):
        go(cond, partial.at[at], running.at[at + 1], at_run + at + 1, row_to=row + 1)

    def run_left(cond, at):
        go(cond, partial.at[at], running.at[at], at_run + at, row_to=row - 1)

    def add_running(at, slot):
        def rows_of(index, carry):
            down = pl.ds(pl.multiple_of(index * 16, 16), 16)
            partial[at, down] = partial[at, down] + running[slot, down]
            return carry

        lax.fori_loop(0, block // 16, rows_of, 0)

    for step in reversed(range(1, rows)):

        def one_side(index, carry, step=step):
            at = row + step * (1 - 2 * index)

            @pl.when(jnp.logical_and(at >= 0, at < rows))
            def _():
                query_part(at)

            return carry

        lax.fori_loop(0, 2, one_side, 0)
        run_right(jnp.logical_and(row == 0, row + step < rows), row + step)
        run_left(jnp.logical_and(row == rows - 1, row >= step), row - step)

    def finish_piece(at):
        def rows_of(index, carry):
            down = pl.ds(pl.multiple_of(index * 16, 16), 16)
            value = split[col, at, down] + inbound[at, down]
            piece[at, down] = value.astype(piece.dtype)
            return carry

        lax.fori_loop(0, block // 16, rows_of, 0)

    def columns_of(source, side):
        start = source % per_col * width + side * features
        return pl.ds(pl.multiple_of(start, features), features)

    def return_piece(cond, at):
        go(
            both(cond, owner == col),
            piece.at[at],
            token_grad_out.at[:, columns_of(row, col)],
            at_piece + row,
            row_to=at,
        )
        go(both(cond, owner != col), piece.at[at], landed.at[row], at_piece + row, row_to=at)

    for step in range(rows):
        sides = [(row - step, row >= step), (row + step, row + step < rows)]
        for at, cond in sides[: 1 if step == 0 else 2]:
            arrived(cond, inbound.at[at], at_part + at)

            def finish(at=at):
                finish_piece(at)

            where(cond, finish)
            if step:
                return_piece(cond, at)
    own_piece = load(owner == col, piece.at[row], token_grad_out.at[:, columns_of(row, col)])
    go(
        owner != col,
        piece.at[row],
        token_grad_out.at[:, columns_of(row, col)],
        at_final + row,
        col_to=other,
    )

    product_tiles = out_width // min(WIDE, out_width)
    product_tile = out_width // product_tiles

    def gradient(step):
        if step:
            slab = slabs[step - 1].reshape(rows * block, owned)
        else:
            across = pl.ds(pl.multiple_of(depth * owned, owned), owned)
            slab = line[:, :, across].reshape(rows * block, owned)
        turned[...] = slab.T

        def tile_of(index, carry):
            across = pl.ds(pl.multiple_of(index * product_tile, product_tile), product_tile)
            value = jnp.dot(
                turned[...],
                cots[step, :, :, across].reshape(rows * block, product_tile),
                preferred_element_type=jnp.float32,
            )
            product[:, across] = value + product[:, across] if step else value
            return carry

        lax.fori_loop(0, product_tiles, tile_of, 0)

    def wait_spread(step):
        arrived(None, slabs.at[step - 1], at_slab + step)
        if step not in stored:
            for at in range(rows):
                arrived(None, cots.at[step, at], at_spread + step * rows + at)

    def run_step(step):
        for cond, at, slot, onward in (
            (jnp.logical_and(row > 0, row + step < rows), row + step, row + step + 1, run_right),
            (jnp.logical_and(row < rows - 1, row >= step), row - step, row - step, run_left),
        ):
            arrived(cond, running.at[slot], at_run + slot)

            def add(at=at, slot=slot):
                add_running(at, slot)

            where(cond, add)
            onward(cond, at)

    gradient(0)
    query_part(row)
    for step in range(1, depths):
        wait_spread(step)
        gradient(step)
        if step == 1:
            for far in reversed(range(2, rows)):
                run_step(far)

    send_rows = owned // SEND_PARTS

    def weight_rows(at, part):
        start = at * owned + part * send_rows
        return pl.ds(pl.multiple_of(start, send_rows), send_rows)

    saved = []
    for part in range(STATE_PARTS):
        slot = part % 2
        for copy in state_copies(part):
            copy.wait()
        if part >= 2:
            for copy in result_copies(part - 2):
                copy.wait()

        def rows_of(index, carry, part=part, slot=slot):
            down = pl.ds(pl.multiple_of(index * 8, 8), 8)
            whole = pl.ds(pl.multiple_of(part * part_rows + index * 8, 8), 8)
            grad = product[whole] * grad_scale
            new_first = beta_one * states[slot, 1, down] + (1.0 - beta_one) * grad
            new_second = beta_two * states[slot, 2, down] + (1.0 - beta_two) * grad * grad
            step_value = new_first / bias_one / (jnp.sqrt(new_second / bias_two) + adam_eps)
            old = states[slot, 0, down]
            results[slot, 0, down] = old - learn_rate * (step_value + decay_rate * old)
            results[slot, 1, down] = new_first
            results[slot, 2, down] = new_second
            return carry

        lax.fori_loop(0, part_rows // 8, rows_of, 0)

        def rounded(index, carry, part=part, slot=slot):
            down = pl.ds(pl.multiple_of(index * 16, 16), 16)
            whole = pl.ds(pl.multiple_of(part * part_rows + index * 16, 16), 16)
            shard[whole] = results[slot, 0, down].astype(shard.dtype)
            return carry

        lax.fori_loop(0, part_rows // 16, rounded, 0)
        for copy in result_copies(part):
            copy.start()
        if part + 2 < STATE_PARTS:
            for copy in state_copies(part + 2):
                copy.start()
        if (part + 1) % (STATE_PARTS // SEND_PARTS) == 0:
            sent = part // (STATE_PARTS // SEND_PARTS)
            source = shard.at[pl.ds(sent * send_rows, send_rows)]
            for single in reversed(singles):
                place = at_weight + single * SEND_PARTS + sent
                if single in stored:
                    target = relayed.at[stored.index(single), pl.ds(sent * send_rows, send_rows)]
                else:
                    target = weight_out.at[weight_rows(depth, sent)]
                go(None, source, target, place, depth_to=flip(depth, single))
            saved.append(load(None, source, weight_out.at[weight_rows(depth, sent)]))

    if rows > 1:
        run_step(1)

    for step in range(1, rows):
        for at, cond in ((row - step, row >= step), (row + step, row + step < rows)):
            across = at // per_col != col
            arrived(both(cond, across), landed.at[at], at_piece + at)
            go(
                both(cond, across),
                landed.at[at],
                token_grad_out.at[:, columns_of(at, col)],
                at_final + at,
                col_to=other,
            )

    for sent in range(SEND_PARTS):
        for step in composites:
            have, low = relay_of(step)
            down = pl.ds(sent * send_rows, send_rows)
            source = relayed.at[stored.index(have), down]
            arrived(None, source, at_weight + have * SEND_PARTS + sent)
            place = at_weight + step * SEND_PARTS + sent
            if step in stored:
                target = relayed.at[stored.index(step), down]
            else:
                target = weight_out.at[weight_rows(flip(depth, have), sent)]
            go(None, source, target, place, depth_to=flip(depth, low))
        for have in stored:
            source = relayed.at[stored.index(have), pl.ds(sent * send_rows, send_rows)]
            target = weight_out.at[weight_rows(flip(depth, have), sent)]
            saved.append(load(None, source, target))

    from_left, from_right = row > 0, row < rows - 1
    for cond, slot in ((from_left, row + 1), (from_right, row)):
        arrived(cond, running.at[slot], at_run + slot)

        def add(slot=slot):
            add_running(row, slot)

        where(cond, add)

    def rounded(index, carry):
        down = pl.ds(pl.multiple_of(index * 16, 16), 16)
        query[down] = partial[row, down].astype(query.dtype)
        return carry

    lax.fori_loop(0, block // 16, rounded, 0)
    saved.append(load(None, query, queries_out))
    saved.append(own_piece)

    for part in (STATE_PARTS - 2, STATE_PARTS - 1):
        for copy in result_copies(part):
            copy.wait()
    for at in range(rows):
        away = jnp.logical_and(at != row, at // per_col == col)
        arrived(away, token_grad_out.at[:, columns_of(at, col)], at_piece + at)
        arrived(at // per_col == col, token_grad_out.at[:, columns_of(at, other)], at_final + at)
    for sent in range(SEND_PARTS):
        for step in range(1, depths):
            if step not in stored:
                place = at_weight + step * SEND_PARTS + sent
                arrived(None, weight_out.at[weight_rows(flip(depth, step), sent)], place)
    for cond, wait in saved + pending:
        where(cond, wait)


def step(mesh, tokens, weight, cotangent, master, first_moment, second_moment):
    rows, cols, depths = (mesh.shape[name] for name in ("row", "col", "depth"))
    block, width = tokens.shape[0], weight.shape[0]
    out_width, owned = weight.shape[1], master.shape[0]
    fits = (
        cols == 2
        and rows % 2 == 0
        and depths > 1
        and depths & (depths - 1) == 0
        and block % 32 == 0
        and width % 256 == 0
        and out_width % 128 == 0
        and owned % (16 * STATE_PARTS) == 0
    )
    if not fits:
        return plain(tokens, weight, cotangent, master, first_moment, second_moment)
    small, wide = jnp.bfloat16, jnp.float32
    stored = {relay_of(at)[0] for at in range(1, depths) if at & (at - 1)}
    shapes = [
        ((width, out_width), small),
        ((block // 2, tokens.shape[1]), small),
        ((rows, block, width), small),
        ((depths, rows, block, out_width), small),
        ((depths - 1, rows, block, owned), small),
        ((owned, rows * block), small),
        ((rows, block, out_width), wide),
        ((rows + 1, block, out_width), wide),
        ((2, rows, block, width // 2), wide),
        ((rows, block, width // 2), wide),
        ((rows, block, width // 2), small),
        ((rows, block, width // 2), small),
        ((owned, out_width), wide),
        ((owned, out_width), small),
        ((max(1, len(stored)), owned, out_width), small),
        ((block, out_width), small),
        ((2, 3, owned // STATE_PARTS, out_width), wide),
        ((2, 3, owned // STATE_PARTS, out_width), wide),
    ]
    total_tokens = block * rows * depths
    outs = [
        jax.ShapeDtypeStruct((block, out_width), small),
        jax.ShapeDtypeStruct(tokens.shape, small),
        jax.ShapeDtypeStruct(master.shape, wide),
        jax.ShapeDtypeStruct(master.shape, wide),
        jax.ShapeDtypeStruct(master.shape, wide),
        jax.ShapeDtypeStruct(weight.shape, small),
    ]
    return pl.pallas_call(
        functools.partial(fused, rows, depths, 1.0 / math.sqrt(total_tokens)),
        out_shape=outs,
        in_specs=[pl.BlockSpec(memory_space=pl.ANY)] * 6,
        out_specs=[pl.BlockSpec(memory_space=pl.ANY)] * 6,
        scratch_shapes=[pltpu.VMEM(shape, dtype) for shape, dtype in shapes]
        + [
            pltpu.SemaphoreType.DMA((64,)),
            pltpu.SemaphoreType.DMA((160,)),
            pltpu.SemaphoreType.DMA((96,)),
        ],
        compiler_params=pltpu.CompilerParams(
            collective_id=0, has_side_effects=True, vmem_limit_bytes=66_000_000
        ),
    )(tokens, weight, cotangent, master, first_moment, second_moment)


def solution(mesh):
    in_specs = (
        P(("row", "depth"), "col"),
        P("row", "col"),
        P(("row", "depth"), "col"),
        P(("row", "depth"), "col"),
        P(("row", "depth"), "col"),
        P(("row", "depth"), "col"),
    )
    out_specs = (
        P(("row", "depth"), "col"),
        P(("row", "depth"), "col"),
        P(("row", "depth"), "col"),
        P(("row", "depth"), "col"),
        P(("row", "depth"), "col"),
        P("row", "col"),
    )
    return jax.shard_map(functools.partial(step, mesh), mesh=mesh, in_specs=in_specs, out_specs=out_specs, check_vma=False)
```

```python
import functools
import itertools
import math

import jax
import jax.numpy as jnp
from jax import lax
from jax.experimental import pallas as pl
from jax.experimental.pallas import tpu as pltpu
from jax.sharding import PartitionSpec as P

beta_one = 0.9
beta_two = 0.95
learn_rate = 0.02
decay_rate = 0.1
adam_eps = 1e-08
bias_one = 1.0 - 0.9**50
bias_two = 1.0 - 0.95**50


def swap(value, axis, step):
    size = lax.axis_size(axis)
    return lax.ppermute(value, axis, [(i, i ^ step) for i in range(size)])


def spread(value, axis):
    pieces = [value]
    for step in range(1, lax.axis_size(axis)):
        top = 1 << (step.bit_length() - 1)
        low = step & -step
        pieces.append(swap(pieces[step - low], axis, low) if step != top else swap(value, axis, step))
    return pieces


def in_order(pieces, axis, dim):
    me = lax.axis_index(axis)
    size = pieces[0].shape[dim]
    shape = list(pieces[0].shape)
    shape[dim] = size * len(pieces)
    whole = jnp.zeros(shape, pieces[0].dtype)
    for step, piece in enumerate(pieces):
        whole = lax.dynamic_update_slice_in_dim(whole, piece, (me ^ step) * size, dim)
    return whole


def plain(tokens, weight, cotangent, master, first_moment, second_moment):
    rows, cols, depths = lax.axis_size("row"), lax.axis_size("col"), lax.axis_size("depth")
    col_at, depth_at = lax.axis_index("col"), lax.axis_index("depth")
    block = tokens.shape[0]
    total_tokens = block * rows * depths
    grad_scale = 1.0 / math.sqrt(total_tokens)
    full_rows = in_order(spread(tokens, "col"), "col", 1)
    line_cotangent = lax.all_gather(cotangent, "row", axis=0, tiled=True)
    line_tokens = lax.all_to_all(full_rows, "row", split_axis=1, concat_axis=0, tiled=True)
    features = weight.shape[0] // cols
    parts = []
    for step in reversed(range(cols)):
        panel = lax.dynamic_slice_in_dim(weight, (col_at ^ step) * features, features, 0)
        part = lax.dot_general(
            line_cotangent, panel, (((1,), (1,)), ((), ())), preferred_element_type=jnp.float32
        )
        parts.append(swap(part, "col", step) if step else part)
    piece = sum(parts[1:], parts[0]).astype(jnp.bfloat16)
    partial_queries = jnp.dot(line_tokens, weight, preferred_element_type=jnp.float32)
    queries = lax.psum_scatter(partial_queries, "row", scatter_dimension=0, tiled=True).astype(
        jnp.bfloat16
    )
    piece = lax.all_to_all(
        piece.reshape(rows, block, -1), "row", split_axis=0, concat_axis=0, tiled=True
    )
    piece = lax.all_to_all(
        piece.reshape(cols, rows // cols, block, -1), "col", split_axis=0, concat_axis=0, tiled=True
    )
    token_grad = piece.transpose(2, 1, 0, 3).reshape(tokens.shape)
    shard = line_tokens.shape[1] // depths
    product = 0.0
    for step, other_cotangent in enumerate(spread(line_cotangent, "depth")):
        slab = lax.dynamic_slice_in_dim(line_tokens, (depth_at ^ step) * shard, shard, 1)
        slab = swap(slab, "depth", step) if step else slab
        product = product + lax.dot_general(
            slab, other_cotangent, (((0,), (0,)), ((), ())), preferred_element_type=jnp.float32
        )
    grad = product * grad_scale
    new_first = beta_one * first_moment + (1.0 - beta_one) * grad
    new_second = beta_two * second_moment + (1.0 - beta_two) * grad * grad
    step_value = new_first / bias_one / (jnp.sqrt(new_second / bias_two) + adam_eps)
    new_master = master - learn_rate * (step_value + decay_rate * master)
    shard_weight = new_master.astype(jnp.bfloat16)
    new_weight = in_order(spread(shard_weight, "depth"), "depth", 0)
    return (queries, token_grad, new_master, new_first, new_second, new_weight)


MESH = pl.DeviceIdType.MESH
WIDE = 512
STATE_PARTS = 8
SEND_PARTS = 4
VMEM_LIMIT = 41_000_000


def flip(index, step):
    for bit in range(step.bit_length()):
        if step >> bit & 1:
            index = index + (1 << bit) - 2 * (1 << bit) * (index // (1 << bit) % 2)
    return index


def relay_of(step):
    low = step & -step
    return step - low, low


def fused(
    rows,
    depths,
    grad_scale,
    tokens_hbm,
    weight_hbm,
    cotangent_hbm,
    master_hbm,
    first_hbm,
    second_hbm,
    query,
    token_grad,
    product,
    first,
    second,
    pool,
    weight,
    early,
    line,
    slabs,
    turned,
    partial,
    running,
    split,
    inbound,
    piece,
    landed,
    masters,
    local_sem,
    send_sem,
    recv_sem,
    ready_sem,
):
    row, col, depth = lax.axis_index("row"), lax.axis_index("col"), lax.axis_index("depth")
    other = 1 - col
    block, width = line.shape[1], line.shape[2]
    half = block // 2
    features = width // 2
    out_width = weight.shape[1]
    owned = product.shape[0]
    per_col = rows // 2
    singles = [1 << bit for bit in range(depths.bit_length() - 1)]
    composites = [step for step in range(1, depths) if step & (step - 1)]
    stored = sorted({relay_of(step)[0] for step in composites})

    sends = itertools.count()
    locals_ = itertools.count()
    places = itertools.count()
    pending, pooled = [], []

    def slots(count):
        return [next(places) for _ in range(count)][0]

    at_early = slots(per_col)
    at_line = slots(rows)
    at_cross = slots(rows)
    at_cot = slots(rows)
    at_spread = slots(depths * rows)
    at_part = slots(rows)
    at_piece = slots(rows)
    at_final = slots(rows)
    at_run = slots(2 * (rows + 1))
    at_slab = slots(depths)
    at_pair = slots(depths)
    at_weight = slots(depths * SEND_PARTS)

    def where(cond, act):
        if cond is None:
            act()
        else:
            pl.when(cond)(act)

    def both(one, two):
        return two if one is None else jnp.logical_and(one, two)

    def go(
        cond, source, target, place, row_to=None, col_to=None, depth_to=None, from_pool=False
    ):
        peer = (
            row if row_to is None else row_to,
            col if col_to is None else col_to,
            depth if depth_to is None else depth_to,
        )
        copy = pltpu.make_async_remote_copy(
            src_ref=source,
            dst_ref=target,
            send_sem=send_sem.at[next(sends)],
            recv_sem=recv_sem.at[place],
            device_id=peer,
            device_id_type=MESH,
        )
        where(cond, copy.start)
        (pooled if from_pool else pending).append((cond, copy.wait_send))

    def arrived(cond, target, place):
        copy = pltpu.make_async_remote_copy(
            src_ref=target,
            dst_ref=target,
            send_sem=send_sem.at[0],
            recv_sem=recv_sem.at[place],
            device_id=(row, other, depth),
            device_id_type=MESH,
        )
        where(cond, copy.wait_recv)

    def load(cond, source, target):
        copy = pltpu.make_async_copy(source, target, local_sem.at[next(locals_)])
        where(cond, copy.start)
        return cond, copy.wait

    def cot_rows(step, at, count=1):
        start = (step * rows + at) * block
        return pl.ds(pl.multiple_of(start, block), count * block)

    with jax.named_scope("barrier"):
        barrier = pltpu.get_barrier_semaphore()
        peers = [((row + step) % rows, col, depth) for step in range(1, rows)]
        peers += [(row, other, depth)]
        peers += [(row, col, flip(depth, step)) for step in range(1, depths)]
        for peer in peers:
            pl.semaphore_signal(barrier, inc=1, device_id=peer, device_id_type=MESH)
        pl.semaphore_wait(barrier, len(peers))

    mine = pl.ds(pl.multiple_of(col * half, half), half)
    theirs = pl.ds(pl.multiple_of(other * half, half), half)
    owner = row // per_col

    def features_of(at):
        return pl.ds(pl.multiple_of(at % per_col * width, width), width)

    near, far = owner == col, owner != col

    def block_at(index):
        return pl.ds(index * width, width)

    for index in range(per_col):
        go(
            None,
            tokens_hbm.at[theirs, block_at(index)],
            early.at[:, block_at(index)],
            at_early + index,
            col_to=other,
        )
    go(
        near,
        tokens_hbm.at[mine, features_of(row)],
        line.at[row, mine],
        at_cross + row,
        col_to=other,
    )
    for index in range(per_col):
        there = col * per_col + index
        go(
            there != row,
            tokens_hbm.at[mine, block_at(index)],
            line.at[row, mine],
            at_line + row,
            row_to=there,
        )
    right, left = row + 1 < rows, row >= 1
    go(right, cotangent_hbm, pool.at[cot_rows(0, row)], at_cot + row, row_to=row + 1)
    go(left, cotangent_hbm, pool.at[cot_rows(0, row)], at_cot + row, row_to=row - 1)
    for step in reversed(singles):
        go(
            None,
            cotangent_hbm,
            pool.at[cot_rows(step, row)],
            at_spread + step * rows + row,
            depth_to=flip(depth, step),
        )
    weight_here = load(None, weight_hbm, weight)
    cot_here = load(None, cotangent_hbm, pool.at[cot_rows(0, row)])
    own_tokens = [load(near, tokens_hbm.at[mine, features_of(row)], line.at[row, mine])]
    moments = [load(None, first_hbm, first), load(None, second_hbm, second)]
    part_rows = owned // STATE_PARTS
    master_sems = [next(locals_) for _ in range(2)]

    def master_in(part):
        return pltpu.make_async_copy(
            master_hbm.at[pl.ds(part * part_rows, part_rows)],
            masters.at[part % 2],
            local_sem.at[master_sems[part % 2]],
        )

    for part in range(2):
        master_in(part).start()

    with jax.named_scope("early"):
        for index in range(per_col):
            there = other * per_col + index
            arrived(None, early.at[:, block_at(index)], at_early + index)
            go(
                there != row,
                early.at[:, block_at(index)],
                line.at[row, mine],
                at_line + row,
                row_to=there,
            )
            go(
                there == row,
                early.at[:, block_at(index)],
                line.at[row, mine],
                at_cross + row,
                col_to=other,
            )
        own_tokens.append(load(far, early.at[:, features_of(row)], line.at[row, mine]))

    tiles = width // min(WIDE, features)
    tile = width // tiles

    def gradient_part(at):
        def tile_of(index, carry):
            start = pl.multiple_of(index * tile, tile)
            side = start // features
            value = lax.dot_general(
                pool[cot_rows(0, at)],
                weight[pl.ds(start, tile)],
                (((1,), (1,)), ((), ())),
                preferred_element_type=jnp.float32,
            )
            inside = pl.ds(pl.multiple_of(start % features, tile), tile)
            split[side, at, :, inside] = value
            return carry

        lax.fori_loop(0, tiles, tile_of, 0)

    def send_part(cond, at):
        go(cond, split.at[other, at], inbound.at[at], at_part + at, col_to=other)


    def spread_on(cond, at):
        for step in composites:
            have, low = relay_of(step)
            if step - have == 1:
                arrived(cond, pool.at[cot_rows(have, at)], at_spread + have * rows + at)
            go(
                cond,
                pool.at[cot_rows(have, at)],
                pool.at[cot_rows(step, at)],
                at_spread + step * rows + at,
                depth_to=flip(depth, low),
                from_pool=True,
            )

    def sides_of(step):
        return [(row - step, row >= step), (row + step, row + step < rows)][: 2 if step else 1]

    def tokens_in(step, which):
        for at, cond in sides_of(step):
            cond = both(cond, which)
            arrived(cond, line.at[at, mine], at_line + at)
            go(cond, line.at[at, mine], line.at[at, mine], at_cross + at, col_to=other)

    def crossed(which):
        for at in range(rows):
            arrived(which, line.at[at, theirs], at_cross + at)

    def slabs_out(which):
        for step in reversed(range(2, depths)):
            there = flip(depth, step)
            go(
                which,
                line.at[:, mine, pl.ds(pl.multiple_of(there * owned, owned), owned)],
                slabs.at[step - 1, :, mine],
                at_slab + step,
                depth_to=there,
            )

    def slabs_across(which):
        for step in range(2, depths):
            arrived(which, slabs.at[step - 1, :, mine], at_slab + step)
            go(
                which,
                slabs.at[step - 1, :, mine],
                slabs.at[step - 1, :, mine],
                at_pair + step,
                col_to=other,
            )

    def cots_in(step):
        onward = [(row + 1 < rows, row + 1), (row >= 1, row - 1)]
        for (at, cond), (more, there) in zip(sides_of(step), onward):
            arrived(cond, pool.at[cot_rows(0, at)], at_cot + at)
            go(
                both(cond, more),
                pool.at[cot_rows(0, at)],
                pool.at[cot_rows(0, at)],
                at_cot + at,
                row_to=there,
                from_pool=True,
            )
            for single in reversed(singles):
                go(
                    cond,
                    pool.at[cot_rows(0, at)],
                    pool.at[cot_rows(single, at)],
                    at_spread + single * rows + at,
                    depth_to=flip(depth, single),
                    from_pool=True,
                )

    def on_sides(step, act, extra=None):
        def one_side(index, carry):
            at = row + step * (2 * index - 1)

            @pl.when(both(extra, jnp.logical_and(at >= 0, at < rows)))
            def _():
                act(at)

            return carry

        lax.fori_loop(0, 2 if step else 1, one_side, 0)

    def parts_make(step):
        on_sides(step, gradient_part)

    def parts_out(step):
        for at, cond in sides_of(step):
            send_part(cond, at)

    def spread_step(step):
        for at, cond in sides_of(step):
            spread_on(cond, at)

    def pieces_home(step):
        for at, cond in sides_of(step):
            arrived(cond, inbound.at[at], at_part + at)
        on_sides(step, finish_piece)
        if step:
            for at, cond in sides_of(step):
                return_piece(cond, at)

    at_end = jnp.logical_or(row == 0, row == rows - 1)
    inside = jnp.logical_and(row > 0, row < rows - 1)

    def run_begin(part, which):
        which = both(which, at_end)
        side = jnp.where(part == 0, owner, 1 - owner)
        for step in reversed(range(1, rows)):
            on_sides(step, lambda at: query_part(at, side), which)
            run_right(both(which, row == 0), row + step, part)
            run_left(both(which, row == rows - 1), row - step, 1 - part)

    query_tiles = out_width // min(WIDE, out_width)
    query_tile = out_width // query_tiles

    def half_of(side):
        return pl.ds(pl.multiple_of(side * half, half), half)

    def query_part(at, side):
        def tile_of(index, carry):
            across = pl.ds(pl.multiple_of(index * query_tile, query_tile), query_tile)
            partial[at, half_of(side), across] = jnp.dot(
                line[at, half_of(side)], weight[:, across], preferred_element_type=jnp.float32
            )
            return carry

        lax.fori_loop(0, query_tiles, tile_of, 0)

    def run_place(slot, side):
        return at_run + side * (rows + 1) + slot

    def run_right(cond, at, side):
        go(
            cond,
            partial.at[at, half_of(side)],
            running.at[at + 1, half_of(side)],
            run_place(at + 1, side),
            row_to=row + 1,
        )

    def run_left(cond, at, side):
        go(
            cond,
            partial.at[at, half_of(side)],
            running.at[at, half_of(side)],
            run_place(at, side),
            row_to=row - 1,
        )

    def run_here(cond, slot, side):
        arrived(cond, running.at[slot, half_of(side)], run_place(slot, side))

    def add_running(at, slot, side):
        def rows_of(index, carry):
            down = pl.ds(pl.multiple_of(side * half + index * 16, 16), 16)
            partial[at, down] = partial[at, down] + running[slot, down]
            return carry

        lax.fori_loop(0, half // 16, rows_of, 0)

    def finish_piece(at):
        def rows_of(index, carry):
            down = pl.ds(pl.multiple_of(index * 16, 16), 16)
            value = split[col, at, down] + inbound[at, down]
            piece[at, down] = value.astype(piece.dtype)
            return carry

        lax.fori_loop(0, block // 16, rows_of, 0)

    def columns_of(source, side):
        start = source % per_col * width + side * features
        return pl.ds(pl.multiple_of(start, features), features)

    def return_piece(cond, at):
        go(
            both(cond, owner == col),
            piece.at[at],
            token_grad.at[:, columns_of(row, col)],
            at_piece + row,
            row_to=at,
        )
        go(both(cond, owner != col), piece.at[at], landed.at[row], at_piece + row, row_to=at)

    product_tiles = out_width // min(WIDE, out_width)
    product_tile = out_width // product_tiles

    def gradient(step):
        if step:
            slab = slabs[step - 1].reshape(rows * block, owned)
        else:
            across = pl.ds(pl.multiple_of(depth * owned, owned), owned)
            slab = line[:, :, across].reshape(rows * block, owned)
        turned[...] = slab.T

        def tile_of(index, carry):
            across = pl.ds(pl.multiple_of(index * product_tile, product_tile), product_tile)
            value = jnp.dot(
                turned[...],
                pool[cot_rows(step, 0, rows), across],
                preferred_element_type=jnp.float32,
            )
            product[:, across] = value + product[:, across] if step else value
            return carry

        lax.fori_loop(0, product_tiles, tile_of, 0)

    def wait_spread(step):
        if step == 1:
            arrived(None, slabs.at[step - 1], at_slab + step)
        else:
            arrived(None, slabs.at[step - 1, :, theirs], at_pair + step)
        if step not in stored:
            for at in range(rows):
                arrived(None, pool.at[cot_rows(step, at)], at_spread + step * rows + at)

    def run_step(step, part):
        for cond, at, slot, onward, side in (
            (row > 0, row + step, row + step + 1, run_right, part),
            (row < rows - 1, row - step, row - step, run_left, 1 - part),
        ):
            cond = both(cond, jnp.logical_and(at >= 0, at < rows))
            run_here(cond, slot, side)

            def add(at=at, slot=slot, side=side):
                add_running(at, slot, side)

            where(cond, add)
            onward(cond, at, side)


    def named(name, act, *args):
        with jax.named_scope(name):
            act(*args)

    def wait_first():
        weight_here[1]()
        cot_here[1]()

    def wait_own(which):
        cond, wait = own_tokens[0 if which is near else 1]
        where(cond, wait)

    def inner_queries(part):
        side = owner if part == 0 else 1 - owner
        for step in reversed(range(1, rows)):
            on_sides(step, lambda at: query_part(at, side), inside)
        query_part(row, side)

    named("wait_first", wait_first)
    named("make0", parts_make, 0)
    named("spread0", spread_step, 0)
    for step in range(1, rows):
        named(f"near_tokens{step}", tokens_in, step, near)
    named("near_own", wait_own, near)
    named("near_slabs", slabs_out, near)
    named("part0", parts_out, 0)
    named("near_begin", run_begin, 0, near)
    named("cots1", cots_in, 1)
    named("near_across", slabs_across, near)
    for step in range(1, rows):
        named(f"far_tokens{step}", tokens_in, step, far)
    named("far_own", wait_own, far)
    named("far_slabs", slabs_out, far)
    named("far_crossed", crossed, far)
    named("far_begin", run_begin, 0, far)
    named("far_begin2", run_begin, 1, far)
    named("cots2", cots_in, 2)
    named("make1", parts_make, 1)
    named("parts1", parts_out, 1)
    named("spread1", spread_step, 1)
    named("near_crossed", crossed, near)
    named("near_begin2", run_begin, 1, near)
    for step in range(3, rows):
        named(f"cots{step}", cots_in, step)
    named("queries1", inner_queries, 0)
    for step in reversed(range(2, rows)):
        named(f"run{step}_first", run_step, step, 0)
    named("queries2", inner_queries, 1)
    with jax.named_scope("slab1"):
        there = flip(depth, 1)
        across = pl.ds(pl.multiple_of(there * owned, owned), owned)
        go(None, line.at[:, :, across], slabs.at[0], at_slab + 1, depth_to=there)
    named("far_across", slabs_across, far)
    for step in range(2, rows):
        named(f"make{step}", parts_make, step)
        named(f"parts{step}", parts_out, step)
        if step < rows - 1:
            named(f"spread{step}", spread_step, step)
    named("pieces0", pieces_home, 0)
    named("run1_first", run_step, 1, 0)
    named("grad0", gradient, 0)
    named("wait_grad1", wait_spread, 1)
    named("grad1", gradient, 1)
    named("pieces1", pieces_home, 1)
    for step in reversed(range(2, rows)):
        named(f"run{step}_second", run_step, step, 1)
    named("spread_last", spread_step, rows - 1)
    for step in range(2, depths):
        named(f"wait_grad{step}", wait_spread, step)
        named(f"grad{step}", gradient, step)

    with jax.named_scope("ready"):
        for cond, wait in pooled:
            where(cond, wait)
        for index, single in enumerate(singles):
            pl.semaphore_signal(
                ready_sem.at[index],
                inc=1,
                device_id=(row, col, flip(depth, single)),
                device_id_type=MESH,
            )
        for _, wait in moments:
            wait()

    send_rows = owned // SEND_PARTS

    def weight_rows(at, part):
        start = at * owned + part * send_rows
        return pl.ds(pl.multiple_of(start, send_rows), send_rows)

    def optimize(part):
        master_in(part).wait()

        def rows_of(index, carry):
            down = pl.ds(pl.multiple_of(index * 16, 16), 16)
            whole = pl.ds(pl.multiple_of(part * part_rows + index * 16, 16), 16)
            kept = pl.ds(pl.multiple_of(depth * owned + part * part_rows + index * 16, 16), 16)
            grad = product[whole] * grad_scale
            new_first = beta_one * first[whole] + (1.0 - beta_one) * grad
            new_second = beta_two * second[whole] + (1.0 - beta_two) * grad * grad
            step_value = new_first / bias_one / (jnp.sqrt(new_second / bias_two) + adam_eps)
            old = masters[part % 2, down]
            new_master = old - learn_rate * (step_value + decay_rate * old)
            product[whole] = new_master
            first[whole] = new_first
            second[whole] = new_second
            pool[kept] = new_master.astype(pool.dtype)
            return carry

        lax.fori_loop(0, part_rows // 16, rows_of, 0)
        if part + 2 < STATE_PARTS:
            master_in(part + 2).start()
        if (part + 1) % (STATE_PARTS // SEND_PARTS):
            return
        sent = part // (STATE_PARTS // SEND_PARTS)
        source = pool.at[weight_rows(depth, sent)]
        for index, single in reversed(list(enumerate(singles))):
            if sent == 0:
                pl.semaphore_wait(ready_sem.at[index], 1)
            go(
                None,
                source,
                source,
                at_weight + single * SEND_PARTS + sent,
                depth_to=flip(depth, single),
            )

    for part in range(STATE_PARTS):
        named(f"optimizer{part}", optimize, part)
        if part % 2 and 2 + part // 2 < rows:
            named(f"pieces{2 + part // 2}", pieces_home, 2 + part // 2)
    for step in range(2 + STATE_PARTS // 2, rows):
        named(f"pieces{step}", pieces_home, step)
    own_piece = load(near, piece.at[row], token_grad.at[:, columns_of(row, col)])
    go(
        far,
        piece.at[row],
        token_grad.at[:, columns_of(row, col)],
        at_final + row,
        col_to=other,
    )
    named("run1_second", run_step, 1, 1)

    with jax.named_scope("landed"):
        for step in range(1, rows):
            for at, cond in ((row - step, row >= step), (row + step, row + step < rows)):
                across = at // per_col != col
                arrived(both(cond, across), landed.at[at], at_piece + at)
                go(
                    both(cond, across),
                    landed.at[at],
                    token_grad.at[:, columns_of(at, col)],
                    at_final + at,
                    col_to=other,
                )

    with jax.named_scope("weights"):
        for sent in range(SEND_PARTS):
            for step in composites:
                have, low = relay_of(step)
                source = pool.at[weight_rows(flip(depth, have), sent)]
                if step - have == 1:
                    arrived(None, source, at_weight + have * SEND_PARTS + sent)
                go(
                    None,
                    source,
                    source,
                    at_weight + step * SEND_PARTS + sent,
                    depth_to=flip(depth, low),
                )

    with jax.named_scope("own_query"):
        from_left, from_right = row > 0, row < rows - 1
        for side in range(2):
            for cond, slot in ((from_left, row + 1), (from_right, row)):
                run_here(cond, slot, side)

                def add(slot=slot, side=side):
                    add_running(row, slot, side)

                where(cond, add)

        def rounded(index, carry):
            down = pl.ds(pl.multiple_of(index * 16, 16), 16)
            query[down] = partial[row, down].astype(query.dtype)
            return carry

        lax.fori_loop(0, block // 16, rounded, 0)

    with jax.named_scope("finish"):
        for at in range(rows):
            away = jnp.logical_and(at != row, at // per_col == col)
            arrived(away, token_grad.at[:, columns_of(at, col)], at_piece + at)
            arrived(at // per_col == col, token_grad.at[:, columns_of(at, other)], at_final + at)
        for sent in range(SEND_PARTS):
            for step in range(1, depths):
                if step not in stored:
                    place = at_weight + step * SEND_PARTS + sent
                    arrived(None, pool.at[weight_rows(flip(depth, step), sent)], place)
        for cond, wait in [own_piece] + pending:
            where(cond, wait)


def write_out(*refs):
    held, outs, sem = refs[:6], refs[6:12], refs[12]
    copies = []
    for index, (source, target) in enumerate(zip(held, outs)):
        copies.append(
            pltpu.make_async_copy(
                source.at[pl.ds(0, target.shape[0])], target, sem.at[index]
            )
        )
    for copy in copies:
        copy.start()
    for copy in copies:
        copy.wait()


def step(mesh, tokens, weight, cotangent, master, first_moment, second_moment):
    rows, cols, depths = (mesh.shape[name] for name in ("row", "col", "depth"))
    block, width = tokens.shape[0], weight.shape[0]
    out_width, owned = weight.shape[1], master.shape[0]
    fits = (
        cols == 2
        and rows > 2
        and rows % 2 == 0
        and depths > 1
        and depths & (depths - 1) == 0
        and block % 32 == 0
        and width % 256 == 0
        and out_width % 128 == 0
        and owned % (16 * STATE_PARTS) == 0
    )
    if not fits:
        return plain(tokens, weight, cotangent, master, first_moment, second_moment)
    small, wide = jnp.bfloat16, jnp.float32
    pool_rows = max(depths * rows * block, width)
    shapes = [
        ((width, out_width), small),
        ((block // 2, tokens.shape[1]), small),
        ((rows, block, width), small),
        ((depths - 1, rows, block, owned), small),
        ((owned, rows * block), small),
        ((rows, block, out_width), wide),
        ((rows + 1, block, out_width), wide),
        ((2, rows, block, width // 2), wide),
        ((rows, block, width // 2), wide),
        ((rows, block, width // 2), small),
        ((rows, block, width // 2), small),
        ((2, owned // STATE_PARTS, out_width), wide),
    ]
    total_tokens = block * rows * depths
    outs = [
        ((block, out_width), small),
        (tokens.shape, small),
        (master.shape, wide),
        (master.shape, wide),
        (master.shape, wide),
        ((pool_rows, out_width), small),
    ]
    held = pl.pallas_call(
        functools.partial(fused, rows, depths, 1.0 / math.sqrt(total_tokens)),
        out_shape=[pltpu.VMEM(shape, dtype) for shape, dtype in outs],
        in_specs=[pl.BlockSpec(memory_space=pl.ANY)] * 6,
        out_specs=[pl.BlockSpec(memory_space=pltpu.VMEM)] * 6,
        scratch_shapes=[pltpu.VMEM(shape, dtype) for shape, dtype in shapes]
        + [
            pltpu.SemaphoreType.DMA((32,)),
            pltpu.SemaphoreType.DMA((192,)),
            pltpu.SemaphoreType.DMA((112,)),
            pltpu.SemaphoreType.REGULAR((max(1, depths.bit_length() - 1),)),
        ],
        compiler_params=pltpu.CompilerParams(
            collective_id=0, has_side_effects=True, vmem_limit_bytes=VMEM_LIMIT
        ),
    )(tokens, weight, cotangent, master, first_moment, second_moment)
    outs[-1] = (weight.shape, small)
    return pl.pallas_call(
        write_out,
        out_shape=[jax.ShapeDtypeStruct(shape, dtype) for shape, dtype in outs],
        in_specs=[pl.BlockSpec(memory_space=pltpu.VMEM)] * 6,
        out_specs=[pl.BlockSpec(memory_space=pl.ANY)] * 6,
        scratch_shapes=[pltpu.SemaphoreType.DMA((6,))],
        compiler_params=pltpu.CompilerParams(vmem_limit_bytes=1 << 20),
    )(*(pltpu.with_memory_space_constraint(value, pltpu.VMEM) for value in held))


def solution(mesh):
    in_specs = (
        P(("row", "depth"), "col"),
        P("row", "col"),
        P(("row", "depth"), "col"),
        P(("row", "depth"), "col"),
        P(("row", "depth"), "col"),
        P(("row", "depth"), "col"),
    )
    out_specs = (
        P(("row", "depth"), "col"),
        P(("row", "depth"), "col"),
        P(("row", "depth"), "col"),
        P(("row", "depth"), "col"),
        P(("row", "depth"), "col"),
        P("row", "col"),
    )
    return jax.shard_map(functools.partial(step, mesh), mesh=mesh, in_specs=in_specs, out_specs=out_specs, check_vma=False)
```

```python
import functools
import itertools
import math

import jax
import jax.numpy as jnp
from jax import lax
from jax.experimental import pallas as pl
from jax.experimental.pallas import tpu as pltpu
from jax.sharding import PartitionSpec as P

beta_one = 0.9
beta_two = 0.95
learn_rate = 0.02
decay_rate = 0.1
adam_eps = 1e-08
bias_one = 1.0 - 0.9**50
bias_two = 1.0 - 0.95**50


def swap(value, axis, step):
    size = lax.axis_size(axis)
    return lax.ppermute(value, axis, [(i, i ^ step) for i in range(size)])


def spread(value, axis):
    pieces = [value]
    for step in range(1, lax.axis_size(axis)):
        top = 1 << (step.bit_length() - 1)
        low = step & -step
        pieces.append(swap(pieces[step - low], axis, low) if step != top else swap(value, axis, step))
    return pieces


def in_order(pieces, axis, dim):
    me = lax.axis_index(axis)
    size = pieces[0].shape[dim]
    shape = list(pieces[0].shape)
    shape[dim] = size * len(pieces)
    whole = jnp.zeros(shape, pieces[0].dtype)
    for step, piece in enumerate(pieces):
        whole = lax.dynamic_update_slice_in_dim(whole, piece, (me ^ step) * size, dim)
    return whole


def plain(tokens, weight, cotangent, master, first_moment, second_moment):
    rows, cols, depths = lax.axis_size("row"), lax.axis_size("col"), lax.axis_size("depth")
    col_at, depth_at = lax.axis_index("col"), lax.axis_index("depth")
    block = tokens.shape[0]
    total_tokens = block * rows * depths
    grad_scale = 1.0 / math.sqrt(total_tokens)
    full_rows = in_order(spread(tokens, "col"), "col", 1)
    line_cotangent = lax.all_gather(cotangent, "row", axis=0, tiled=True)
    line_tokens = lax.all_to_all(full_rows, "row", split_axis=1, concat_axis=0, tiled=True)
    features = weight.shape[0] // cols
    parts = []
    for step in reversed(range(cols)):
        panel = lax.dynamic_slice_in_dim(weight, (col_at ^ step) * features, features, 0)
        part = lax.dot_general(
            line_cotangent, panel, (((1,), (1,)), ((), ())), preferred_element_type=jnp.float32
        )
        parts.append(swap(part, "col", step) if step else part)
    piece = sum(parts[1:], parts[0]).astype(jnp.bfloat16)
    partial_queries = jnp.dot(line_tokens, weight, preferred_element_type=jnp.float32)
    queries = lax.psum_scatter(partial_queries, "row", scatter_dimension=0, tiled=True).astype(
        jnp.bfloat16
    )
    piece = lax.all_to_all(
        piece.reshape(rows, block, -1), "row", split_axis=0, concat_axis=0, tiled=True
    )
    piece = lax.all_to_all(
        piece.reshape(cols, rows // cols, block, -1), "col", split_axis=0, concat_axis=0, tiled=True
    )
    token_grad = piece.transpose(2, 1, 0, 3).reshape(tokens.shape)
    shard = line_tokens.shape[1] // depths
    product = 0.0
    for step, other_cotangent in enumerate(spread(line_cotangent, "depth")):
        slab = lax.dynamic_slice_in_dim(line_tokens, (depth_at ^ step) * shard, shard, 1)
        slab = swap(slab, "depth", step) if step else slab
        product = product + lax.dot_general(
            slab, other_cotangent, (((0,), (0,)), ((), ())), preferred_element_type=jnp.float32
        )
    grad = product * grad_scale
    new_first = beta_one * first_moment + (1.0 - beta_one) * grad
    new_second = beta_two * second_moment + (1.0 - beta_two) * grad * grad
    step_value = new_first / bias_one / (jnp.sqrt(new_second / bias_two) + adam_eps)
    new_master = master - learn_rate * (step_value + decay_rate * master)
    shard_weight = new_master.astype(jnp.bfloat16)
    new_weight = in_order(spread(shard_weight, "depth"), "depth", 0)
    return (queries, token_grad, new_master, new_first, new_second, new_weight)


MESH = pl.DeviceIdType.MESH
WIDE = 512
STATE_PARTS = 8
SEND_PARTS = 4
VMEM_LIMIT = 41_000_000


def flip(index, step):
    for bit in range(step.bit_length()):
        if step >> bit & 1:
            index = index + (1 << bit) - 2 * (1 << bit) * (index // (1 << bit) % 2)
    return index


def relay_of(step):
    low = step & -step
    return step - low, low


def fused(
    rows,
    depths,
    grad_scale,
    tokens_hbm,
    weight_hbm,
    cotangent_hbm,
    master_hbm,
    first_hbm,
    second_hbm,
    query,
    token_grad,
    product,
    first,
    second,
    pool,
    weight,
    early,
    line,
    slabs,
    turned,
    partial,
    running,
    split,
    inbound,
    piece,
    landed,
    masters,
    local_sem,
    send_sem,
    recv_sem,
    ready_sem,
):
    row, col, depth = lax.axis_index("row"), lax.axis_index("col"), lax.axis_index("depth")
    other = 1 - col
    block, width = line.shape[1], line.shape[2]
    half = block // 2
    features = width // 2
    out_width = weight.shape[1]
    owned = product.shape[0]
    per_col = rows // 2
    singles = [1 << bit for bit in range(depths.bit_length() - 1)]
    composites = [step for step in range(1, depths) if step & (step - 1)]
    stored = sorted({relay_of(step)[0] for step in composites})

    sends = itertools.count()
    locals_ = itertools.count()
    places = itertools.count()
    pending, pooled = [], []

    def slots(count):
        return [next(places) for _ in range(count)][0]

    at_early = slots(per_col)
    at_line = slots(rows)
    at_cross = slots(rows)
    at_cot = slots(rows)
    at_spread = slots(depths * rows)
    at_part = slots(rows)
    at_piece = slots(rows)
    at_final = slots(rows)
    at_run = slots(2 * (rows + 1))
    at_slab = slots(depths)
    at_pair = slots(depths)
    at_weight = slots(depths * SEND_PARTS)

    def where(cond, act):
        if cond is None:
            act()
        else:
            pl.when(cond)(act)

    def both(one, two):
        return two if one is None else jnp.logical_and(one, two)

    def go(
        cond, source, target, place, row_to=None, col_to=None, depth_to=None, from_pool=False
    ):
        peer = (
            row if row_to is None else row_to,
            col if col_to is None else col_to,
            depth if depth_to is None else depth_to,
        )
        copy = pltpu.make_async_remote_copy(
            src_ref=source,
            dst_ref=target,
            send_sem=send_sem.at[next(sends)],
            recv_sem=recv_sem.at[place],
            device_id=peer,
            device_id_type=MESH,
        )
        where(cond, copy.start)
        (pooled if from_pool else pending).append((cond, copy.wait_send))

    def arrived(cond, target, place):
        copy = pltpu.make_async_remote_copy(
            src_ref=target,
            dst_ref=target,
            send_sem=send_sem.at[0],
            recv_sem=recv_sem.at[place],
            device_id=(row, other, depth),
            device_id_type=MESH,
        )
        where(cond, copy.wait_recv)

    def load(cond, source, target):
        copy = pltpu.make_async_copy(source, target, local_sem.at[next(locals_)])
        where(cond, copy.start)
        return cond, copy.wait

    def cot_rows(step, at, count=1):
        start = (step * rows + at) * block
        return pl.ds(pl.multiple_of(start, block), count * block)

    with jax.named_scope("barrier"):
        barrier = pltpu.get_barrier_semaphore()
        peers = [((row + step) % rows, col, depth) for step in range(1, rows)]
        peers += [(row, other, depth)]
        peers += [(row, col, flip(depth, step)) for step in range(1, depths)]
        for peer in peers:
            pl.semaphore_signal(barrier, inc=1, device_id=peer, device_id_type=MESH)
        pl.semaphore_wait(barrier, len(peers))

    mine = pl.ds(pl.multiple_of(col * half, half), half)
    theirs = pl.ds(pl.multiple_of(other * half, half), half)
    owner = row // per_col

    def features_of(at):
        return pl.ds(pl.multiple_of(at % per_col * width, width), width)

    near, far = owner == col, owner != col

    def block_at(index):
        return pl.ds(index * width, width)

    for index in range(per_col):
        go(
            None,
            tokens_hbm.at[theirs, block_at(index)],
            early.at[:, block_at(index)],
            at_early + index,
            col_to=other,
        )
    go(
        near,
        tokens_hbm.at[mine, features_of(row)],
        line.at[row, mine],
        at_cross + row,
        col_to=other,
    )
    for index in range(per_col):
        there = col * per_col + index
        go(
            there != row,
            tokens_hbm.at[mine, block_at(index)],
            line.at[row, mine],
            at_line + row,
            row_to=there,
        )
    right, left = row + 1 < rows, row >= 1
    go(right, cotangent_hbm, pool.at[cot_rows(0, row)], at_cot + row, row_to=row + 1)
    go(left, cotangent_hbm, pool.at[cot_rows(0, row)], at_cot + row, row_to=row - 1)
    for step in reversed(singles):
        go(
            None,
            cotangent_hbm,
            pool.at[cot_rows(step, row)],
            at_spread + step * rows + row,
            depth_to=flip(depth, step),
        )
    weight_here = load(None, weight_hbm, weight)
    cot_here = load(None, cotangent_hbm, pool.at[cot_rows(0, row)])
    own_tokens = [load(near, tokens_hbm.at[mine, features_of(row)], line.at[row, mine])]
    moments = [load(None, first_hbm, first), load(None, second_hbm, second)]
    part_rows = owned // STATE_PARTS
    master_sems = [next(locals_) for _ in range(2)]

    def master_in(part):
        return pltpu.make_async_copy(
            master_hbm.at[pl.ds(part * part_rows, part_rows)],
            masters.at[part % 2],
            local_sem.at[master_sems[part % 2]],
        )

    for part in range(2):
        master_in(part).start()

    with jax.named_scope("early"):
        for index in range(per_col):
            there = other * per_col + index
            arrived(None, early.at[:, block_at(index)], at_early + index)
            go(
                there != row,
                early.at[:, block_at(index)],
                line.at[row, mine],
                at_line + row,
                row_to=there,
            )
            go(
                there == row,
                early.at[:, block_at(index)],
                line.at[row, mine],
                at_cross + row,
                col_to=other,
            )
        own_tokens.append(load(far, early.at[:, features_of(row)], line.at[row, mine]))

    tiles = width // min(WIDE, features)
    tile = width // tiles

    def gradient_part(at):
        def tile_of(index, carry):
            start = pl.multiple_of(index * tile, tile)
            side = start // features
            value = lax.dot_general(
                pool[cot_rows(0, at)],
                weight[pl.ds(start, tile)],
                (((1,), (1,)), ((), ())),
                preferred_element_type=jnp.float32,
            )
            inside = pl.ds(pl.multiple_of(start % features, tile), tile)
            split[side, at, :, inside] = value
            return carry

        lax.fori_loop(0, tiles, tile_of, 0)

    def send_part(cond, at):
        go(cond, split.at[other, at], inbound.at[at], at_part + at, col_to=other)


    def spread_on(cond, at):
        for step in composites:
            have, low = relay_of(step)
            if step - have == 1:
                arrived(cond, pool.at[cot_rows(have, at)], at_spread + have * rows + at)
            go(
                cond,
                pool.at[cot_rows(have, at)],
                pool.at[cot_rows(step, at)],
                at_spread + step * rows + at,
                depth_to=flip(depth, low),
                from_pool=True,
            )

    def sides_of(step):
        return [(row - step, row >= step), (row + step, row + step < rows)][: 2 if step else 1]

    def tokens_in(step, which):
        for at, cond in sides_of(step):
            cond = both(cond, which)
            arrived(cond, line.at[at, mine], at_line + at)
            go(cond, line.at[at, mine], line.at[at, mine], at_cross + at, col_to=other)

    def crossed(which, step):
        for at, cond in sides_of(step):
            arrived(both(cond, which), line.at[at, theirs], at_cross + at)

    def slabs_out(which, tokens, place):
        for step in reversed(range(2, depths)):
            there = flip(depth, step)
            go(
                which,
                line.at[:, tokens, pl.ds(pl.multiple_of(there * owned, owned), owned)],
                slabs.at[step - 1, :, tokens],
                place + step,
                depth_to=there,
            )

    def cots_in(step):
        onward = [(row + 1 < rows, row + 1), (row >= 1, row - 1)]
        for (at, cond), (more, there) in zip(sides_of(step), onward):
            arrived(cond, pool.at[cot_rows(0, at)], at_cot + at)
            go(
                both(cond, more),
                pool.at[cot_rows(0, at)],
                pool.at[cot_rows(0, at)],
                at_cot + at,
                row_to=there,
                from_pool=True,
            )
            for single in reversed(singles):
                go(
                    cond,
                    pool.at[cot_rows(0, at)],
                    pool.at[cot_rows(single, at)],
                    at_spread + single * rows + at,
                    depth_to=flip(depth, single),
                    from_pool=True,
                )

    def on_sides(step, act, extra=None):
        def one_side(index, carry):
            at = row + step * (2 * index - 1)

            @pl.when(both(extra, jnp.logical_and(at >= 0, at < rows)))
            def _():
                act(at)

            return carry

        lax.fori_loop(0, 2 if step else 1, one_side, 0)

    def parts_make(step):
        on_sides(step, gradient_part)

    def parts_out(step):
        for at, cond in sides_of(step):
            send_part(cond, at)

    def spread_step(step):
        for at, cond in sides_of(step):
            spread_on(cond, at)

    def pieces_home(step, which=None):
        for at, cond in sides_of(step):
            arrived(both(which, cond), inbound.at[at], at_part + at)
        on_sides(step, finish_piece, which)
        if step:
            for at, cond in sides_of(step):
                return_piece(both(which, cond), at)

    at_end = jnp.logical_or(row == 0, row == rows - 1)
    inside = jnp.logical_and(row > 0, row < rows - 1)

    def run_begin(part, which, step, held=False):
        inner = both(which, at_end)
        side = jnp.where(part == 0, owner, 1 - owner)
        on_sides(step, lambda at: query_part(at, side), inner)
        if not held:
            run_out(part, which, step)

    def run_out(part, which, step):
        run_right(both(which, row == 0), row + step, part)
        run_left(both(which, row == rows - 1), row - step, 1 - part)

    query_tiles = out_width // min(WIDE, out_width)
    query_tile = out_width // query_tiles

    def half_of(side):
        return pl.ds(pl.multiple_of(side * half, half), half)

    def query_part(at, side):
        def tile_of(index, carry):
            across = pl.ds(pl.multiple_of(index * query_tile, query_tile), query_tile)
            partial[at, half_of(side), across] = jnp.dot(
                line[at, half_of(side)], weight[:, across], preferred_element_type=jnp.float32
            )
            return carry

        lax.fori_loop(0, query_tiles, tile_of, 0)

    def run_place(slot, side):
        return at_run + side * (rows + 1) + slot

    def run_right(cond, at, side):
        go(
            cond,
            partial.at[at, half_of(side)],
            running.at[at + 1, half_of(side)],
            run_place(at + 1, side),
            row_to=row + 1,
        )

    def run_left(cond, at, side):
        go(
            cond,
            partial.at[at, half_of(side)],
            running.at[at, half_of(side)],
            run_place(at, side),
            row_to=row - 1,
        )

    def run_here(cond, slot, side):
        arrived(cond, running.at[slot, half_of(side)], run_place(slot, side))

    def add_running(at, slot, side):
        def rows_of(index, carry):
            down = pl.ds(pl.multiple_of(side * half + index * 16, 16), 16)
            partial[at, down] = partial[at, down] + running[slot, down]
            return carry

        lax.fori_loop(0, half // 16, rows_of, 0)

    def finish_piece(at):
        def rows_of(index, carry):
            down = pl.ds(pl.multiple_of(index * 16, 16), 16)
            value = split[col, at, down] + inbound[at, down]
            piece[at, down] = value.astype(piece.dtype)
            return carry

        lax.fori_loop(0, block // 16, rows_of, 0)

    def columns_of(source, side):
        start = source % per_col * width + side * features
        return pl.ds(pl.multiple_of(start, features), features)

    def return_piece(cond, at):
        go(
            both(cond, owner == col),
            piece.at[at],
            token_grad.at[:, columns_of(row, col)],
            at_piece + row,
            row_to=at,
        )
        go(both(cond, owner != col), piece.at[at], landed.at[row], at_piece + row, row_to=at)

    product_tiles = out_width // min(WIDE, out_width)
    product_tile = out_width // product_tiles

    def gradient(step):
        if step:
            slab = slabs[step - 1].reshape(rows * block, owned)
        else:
            across = pl.ds(pl.multiple_of(depth * owned, owned), owned)
            slab = line[:, :, across].reshape(rows * block, owned)
        turned[...] = slab.T

        def tile_of(index, carry):
            across = pl.ds(pl.multiple_of(index * product_tile, product_tile), product_tile)
            value = jnp.dot(
                turned[...],
                pool[cot_rows(step, 0, rows), across],
                preferred_element_type=jnp.float32,
            )
            product[:, across] = value + product[:, across] if step else value
            return carry

        lax.fori_loop(0, product_tiles, tile_of, 0)

    def wait_spread(step):
        if step == 1:
            arrived(None, slabs.at[step - 1], at_slab + step)
        else:
            arrived(None, slabs.at[step - 1, :, mine], at_slab + step)
            arrived(None, slabs.at[step - 1, :, theirs], at_pair + step)
        if step not in stored:
            for at in range(rows):
                arrived(None, pool.at[cot_rows(step, at)], at_spread + step * rows + at)

    def run_step(step, part, origin, which=None):
        for cond, at, slot, onward, side, begun in (
            (row > 0, row + step, row + step + 1, run_right, part, col == origin),
            (row < rows - 1, row - step, row - step, run_left, 1 - part, col != origin),
        ):
            cond = both(which, both(begun, both(cond, jnp.logical_and(at >= 0, at < rows))))
            run_here(cond, slot, side)

            def add(at=at, slot=slot, side=side):
                add_running(at, slot, side)

            where(cond, add)
            onward(cond, at, side)

    def named(name, act, *args):
        with jax.named_scope(name):
            act(*args)

    def wait_first():
        weight_here[1]()
        cot_here[1]()

    def wait_own(which):
        cond, wait = own_tokens[0 if which is near else 1]
        where(cond, wait)

    def inner_queries(part):
        side = owner if part == 0 else 1 - owner
        for step in reversed(range(1, rows)):
            on_sides(step, lambda at: query_part(at, side), inside)
        query_part(row, side)

    named("wait_first", wait_first)
    named("make0", parts_make, 0)
    named("spread0", spread_step, 0)
    for step in range(1, rows):
        named(f"near_tokens{step}", tokens_in, step, near)
    named("near_own", wait_own, near)
    named("near_slabs", slabs_out, near, mine, at_slab)
    named("part0", parts_out, 0)
    for step in reversed(range(1, rows)):
        named(f"near_begin{step}", run_begin, 0, near, step)
    named("cots1", cots_in, 1)
    for step in range(1, rows):
        named(f"far_tokens{step}", tokens_in, step, far)
        named(f"far_crossed{step}", crossed, far, step)
        named(f"far_begin{step}", run_begin, 0, far, step)
    named("far_own", wait_own, far)
    named("far_crossed0", crossed, far, 0)
    named("far_slabs", slabs_out, far, mine, at_slab)
    named("far_slabs2", slabs_out, far, theirs, at_pair)
    for step in reversed(range(1, rows)):
        named(f"far_second{step}", run_begin, 1, far, step, step == 1)
    named("queries1", inner_queries, 0)
    for step in reversed(range(2, rows)):
        named(f"run{step}_first", run_step, step, 0, 0, near)
    named("make1", parts_make, 1)
    named("parts1", parts_out, 1)
    named("cots2", cots_in, 2)
    named("run1_far", run_step, 1, 0, 1, far)
    named("run1_near", run_step, 1, 0, 0, near)
    for step in reversed(range(rows)):
        named(f"near_crossed{step}", crossed, near, step)
        if step:
            named(f"near_second{step}", run_begin, 1, near, step, step == 1)
    named("near_slabs2", slabs_out, near, theirs, at_pair)
    named("queries2", inner_queries, 1)
    for step in range(2, rows):
        named(f"run{step}_far", run_step, step, 0, 1, far)
    named("run1_late", run_step, 1, 0, 0, far)
    named("make2", parts_make, 2)
    named("parts2", parts_out, 2)
    named("spread1", spread_step, 1)
    with jax.named_scope("slab1"):
        there = flip(depth, 1)
        across = pl.ds(pl.multiple_of(there * owned, owned), owned)
        go(None, line.at[:, :, across], slabs.at[0], at_slab + 1, depth_to=there)
    for step in range(3, rows):
        named(f"cots{step}", cots_in, step)
        named(f"make{step}", parts_make, step)
        named(f"parts{step}", parts_out, step)
    named("pieces0", pieces_home, 0)
    own_piece = load(near, piece.at[row], token_grad.at[:, columns_of(row, col)])
    go(
        far,
        piece.at[row],
        token_grad.at[:, columns_of(row, col)],
        at_final + row,
        col_to=other,
    )
    named("grad0", gradient, 0)
    named("wait_grad1", wait_spread, 1)
    named("grad1", gradient, 1)
    for step in range(2, rows - 1):
        named(f"spread{step}", spread_step, step)
    early_pieces = jnp.logical_or(near, at_end)
    named("pieces1", pieces_home, 1, early_pieces)
    named("run1_last", run_step, 1, 0, 1, near)
    for step in reversed(range(2, rows)):
        named(f"run{step}_second", run_step, step, 1, 0)
        named(f"run{step}_second2", run_step, step, 1, 1)
    named("spread_last", spread_step, rows - 1)
    for step in range(2, depths):
        named(f"wait_grad{step}", wait_spread, step)
        named(f"grad{step}", gradient, step)

    with jax.named_scope("ready"):
        for cond, wait in pooled:
            where(cond, wait)
        for index, single in enumerate(singles):
            pl.semaphore_signal(
                ready_sem.at[index],
                inc=1,
                device_id=(row, col, flip(depth, single)),
                device_id_type=MESH,
            )
        for _, wait in moments:
            wait()

    send_rows = owned // SEND_PARTS

    def weight_rows(at, part):
        start = at * owned + part * send_rows
        return pl.ds(pl.multiple_of(start, send_rows), send_rows)

    def optimize(part):
        master_in(part).wait()

        def rows_of(index, carry):
            down = pl.ds(pl.multiple_of(index * 16, 16), 16)
            whole = pl.ds(pl.multiple_of(part * part_rows + index * 16, 16), 16)
            kept = pl.ds(pl.multiple_of(depth * owned + part * part_rows + index * 16, 16), 16)
            grad = product[whole] * grad_scale
            new_first = beta_one * first[whole] + (1.0 - beta_one) * grad
            new_second = beta_two * second[whole] + (1.0 - beta_two) * grad * grad
            step_value = new_first / bias_one / (jnp.sqrt(new_second / bias_two) + adam_eps)
            old = masters[part % 2, down]
            new_master = old - learn_rate * (step_value + decay_rate * old)
            product[whole] = new_master
            first[whole] = new_first
            second[whole] = new_second
            pool[kept] = new_master.astype(pool.dtype)
            return carry

        lax.fori_loop(0, part_rows // 16, rows_of, 0)
        if part + 2 < STATE_PARTS:
            master_in(part + 2).start()
        if (part + 1) % (STATE_PARTS // SEND_PARTS):
            return
        sent = part // (STATE_PARTS // SEND_PARTS)
        source = pool.at[weight_rows(depth, sent)]
        for index, single in reversed(list(enumerate(singles))):
            if sent == 0:
                pl.semaphore_wait(ready_sem.at[index], 1)
            go(
                None,
                source,
                source,
                at_weight + single * SEND_PARTS + sent,
                depth_to=flip(depth, single),
            )

    for part in range(STATE_PARTS):
        named(f"optimizer{part}", optimize, part)
    named("pieces1_late", pieces_home, 1, jnp.logical_not(early_pieces))
    named("pieces2", pieces_home, 2)
    named("run1_second", run_step, 1, 1, 0)
    named("run1_second2", run_step, 1, 1, 1)
    for step in range(3, rows):
        named(f"pieces{step}", pieces_home, step)
    named("run_out_last", run_out, 1, None, 1)
    with jax.named_scope("landed"):
        for step in range(1, rows):
            for at, cond in ((row - step, row >= step), (row + step, row + step < rows)):
                across = at // per_col != col
                arrived(both(cond, across), landed.at[at], at_piece + at)
                go(
                    both(cond, across),
                    landed.at[at],
                    token_grad.at[:, columns_of(at, col)],
                    at_final + at,
                    col_to=other,
                )

    with jax.named_scope("weights"):
        for sent in range(SEND_PARTS):
            for step in composites:
                have, low = relay_of(step)
                source = pool.at[weight_rows(flip(depth, have), sent)]
                if step - have == 1:
                    arrived(None, source, at_weight + have * SEND_PARTS + sent)
                go(
                    None,
                    source,
                    source,
                    at_weight + step * SEND_PARTS + sent,
                    depth_to=flip(depth, low),
                )

    with jax.named_scope("own_query"):
        from_left, from_right = row > 0, row < rows - 1
        for side in range(2):
            for cond, slot in ((from_left, row + 1), (from_right, row)):
                run_here(cond, slot, side)

                def add(slot=slot, side=side):
                    add_running(row, slot, side)

                where(cond, add)

        def rounded(index, carry):
            down = pl.ds(pl.multiple_of(index * 16, 16), 16)
            query[down] = partial[row, down].astype(query.dtype)
            return carry

        lax.fori_loop(0, block // 16, rounded, 0)

    with jax.named_scope("finish"):
        for at in range(rows):
            away = jnp.logical_and(at != row, at // per_col == col)
            arrived(away, token_grad.at[:, columns_of(at, col)], at_piece + at)
            arrived(at // per_col == col, token_grad.at[:, columns_of(at, other)], at_final + at)
        for sent in range(SEND_PARTS):
            for step in range(1, depths):
                if step not in stored:
                    place = at_weight + step * SEND_PARTS + sent
                    arrived(None, pool.at[weight_rows(flip(depth, step), sent)], place)
        for cond, wait in [own_piece] + pending:
            where(cond, wait)


def write_out(*refs):
    held, outs, sem = refs[:6], refs[6:12], refs[12]
    copies = []
    for index, (source, target) in enumerate(zip(held, outs)):
        copies.append(
            pltpu.make_async_copy(
                source.at[pl.ds(0, target.shape[0])], target, sem.at[index]
            )
        )
    for copy in copies:
        copy.start()
    for copy in copies:
        copy.wait()


def step(mesh, tokens, weight, cotangent, master, first_moment, second_moment):
    rows, cols, depths = (mesh.shape[name] for name in ("row", "col", "depth"))
    block, width = tokens.shape[0], weight.shape[0]
    out_width, owned = weight.shape[1], master.shape[0]
    fits = (
        cols == 2
        and rows > 2
        and rows % 2 == 0
        and depths > 1
        and depths & (depths - 1) == 0
        and block % 32 == 0
        and width % 256 == 0
        and out_width % 128 == 0
        and owned % (16 * STATE_PARTS) == 0
    )
    if not fits:
        return plain(tokens, weight, cotangent, master, first_moment, second_moment)
    small, wide = jnp.bfloat16, jnp.float32
    pool_rows = max(depths * rows * block, width)
    shapes = [
        ((width, out_width), small),
        ((block // 2, tokens.shape[1]), small),
        ((rows, block, width), small),
        ((depths - 1, rows, block, owned), small),
        ((owned, rows * block), small),
        ((rows, block, out_width), wide),
        ((rows + 1, block, out_width), wide),
        ((2, rows, block, width // 2), wide),
        ((rows, block, width // 2), wide),
        ((rows, block, width // 2), small),
        ((rows, block, width // 2), small),
        ((2, owned // STATE_PARTS, out_width), wide),
    ]
    total_tokens = block * rows * depths
    outs = [
        ((block, out_width), small),
        (tokens.shape, small),
        (master.shape, wide),
        (master.shape, wide),
        (master.shape, wide),
        ((pool_rows, out_width), small),
    ]
    held = pl.pallas_call(
        functools.partial(fused, rows, depths, 1.0 / math.sqrt(total_tokens)),
        out_shape=[pltpu.VMEM(shape, dtype) for shape, dtype in outs],
        in_specs=[pl.BlockSpec(memory_space=pl.ANY)] * 6,
        out_specs=[pl.BlockSpec(memory_space=pltpu.VMEM)] * 6,
        scratch_shapes=[pltpu.VMEM(shape, dtype) for shape, dtype in shapes]
        + [
            pltpu.SemaphoreType.DMA((32,)),
            pltpu.SemaphoreType.DMA((192,)),
            pltpu.SemaphoreType.DMA((112,)),
            pltpu.SemaphoreType.REGULAR((max(1, depths.bit_length() - 1),)),
        ],
        compiler_params=pltpu.CompilerParams(
            collective_id=0, has_side_effects=True, vmem_limit_bytes=VMEM_LIMIT
        ),
    )(tokens, weight, cotangent, master, first_moment, second_moment)
    outs[-1] = (weight.shape, small)
    return pl.pallas_call(
        write_out,
        out_shape=[jax.ShapeDtypeStruct(shape, dtype) for shape, dtype in outs],
        in_specs=[pl.BlockSpec(memory_space=pltpu.VMEM)] * 6,
        out_specs=[pl.BlockSpec(memory_space=pl.ANY)] * 6,
        scratch_shapes=[pltpu.SemaphoreType.DMA((6,))],
        compiler_params=pltpu.CompilerParams(vmem_limit_bytes=1 << 20),
    )(*(pltpu.with_memory_space_constraint(value, pltpu.VMEM) for value in held))


def solution(mesh):
    in_specs = (
        P(("row", "depth"), "col"),
        P("row", "col"),
        P(("row", "depth"), "col"),
        P(("row", "depth"), "col"),
        P(("row", "depth"), "col"),
        P(("row", "depth"), "col"),
    )
    out_specs = (
        P(("row", "depth"), "col"),
        P(("row", "depth"), "col"),
        P(("row", "depth"), "col"),
        P(("row", "depth"), "col"),
        P(("row", "depth"), "col"),
        P("row", "col"),
    )
    return jax.shard_map(functools.partial(step, mesh), mesh=mesh, in_specs=in_specs, out_specs=out_specs, check_vma=False)
```

```python
import functools
import itertools
import math

import jax
import jax.numpy as jnp
from jax import lax
from jax.experimental import pallas as pl
from jax.experimental.pallas import tpu as pltpu
from jax.sharding import PartitionSpec as P

beta_one = 0.9
beta_two = 0.95
learn_rate = 0.02
decay_rate = 0.1
adam_eps = 1e-08
bias_one = 1.0 - 0.9**50
bias_two = 1.0 - 0.95**50


def swap(value, axis, step):
    size = lax.axis_size(axis)
    return lax.ppermute(value, axis, [(i, i ^ step) for i in range(size)])


def spread(value, axis):
    pieces = [value]
    for step in range(1, lax.axis_size(axis)):
        top = 1 << (step.bit_length() - 1)
        low = step & -step
        pieces.append(swap(pieces[step - low], axis, low) if step != top else swap(value, axis, step))
    return pieces


def in_order(pieces, axis, dim):
    me = lax.axis_index(axis)
    size = pieces[0].shape[dim]
    shape = list(pieces[0].shape)
    shape[dim] = size * len(pieces)
    whole = jnp.zeros(shape, pieces[0].dtype)
    for step, piece in enumerate(pieces):
        whole = lax.dynamic_update_slice_in_dim(whole, piece, (me ^ step) * size, dim)
    return whole


def plain(tokens, weight, cotangent, master, first_moment, second_moment):
    rows, cols, depths = lax.axis_size("row"), lax.axis_size("col"), lax.axis_size("depth")
    col_at, depth_at = lax.axis_index("col"), lax.axis_index("depth")
    block = tokens.shape[0]
    total_tokens = block * rows * depths
    grad_scale = 1.0 / math.sqrt(total_tokens)
    full_rows = in_order(spread(tokens, "col"), "col", 1)
    line_cotangent = lax.all_gather(cotangent, "row", axis=0, tiled=True)
    line_tokens = lax.all_to_all(full_rows, "row", split_axis=1, concat_axis=0, tiled=True)
    features = weight.shape[0] // cols
    parts = []
    for step in reversed(range(cols)):
        panel = lax.dynamic_slice_in_dim(weight, (col_at ^ step) * features, features, 0)
        part = lax.dot_general(
            line_cotangent, panel, (((1,), (1,)), ((), ())), preferred_element_type=jnp.float32
        )
        parts.append(swap(part, "col", step) if step else part)
    piece = sum(parts[1:], parts[0]).astype(jnp.bfloat16)
    partial_queries = jnp.dot(line_tokens, weight, preferred_element_type=jnp.float32)
    queries = lax.psum_scatter(partial_queries, "row", scatter_dimension=0, tiled=True).astype(
        jnp.bfloat16
    )
    piece = lax.all_to_all(
        piece.reshape(rows, block, -1), "row", split_axis=0, concat_axis=0, tiled=True
    )
    piece = lax.all_to_all(
        piece.reshape(cols, rows // cols, block, -1), "col", split_axis=0, concat_axis=0, tiled=True
    )
    token_grad = piece.transpose(2, 1, 0, 3).reshape(tokens.shape)
    shard = line_tokens.shape[1] // depths
    product = 0.0
    for step, other_cotangent in enumerate(spread(line_cotangent, "depth")):
        slab = lax.dynamic_slice_in_dim(line_tokens, (depth_at ^ step) * shard, shard, 1)
        slab = swap(slab, "depth", step) if step else slab
        product = product + lax.dot_general(
            slab, other_cotangent, (((0,), (0,)), ((), ())), preferred_element_type=jnp.float32
        )
    grad = product * grad_scale
    new_first = beta_one * first_moment + (1.0 - beta_one) * grad
    new_second = beta_two * second_moment + (1.0 - beta_two) * grad * grad
    step_value = new_first / bias_one / (jnp.sqrt(new_second / bias_two) + adam_eps)
    new_master = master - learn_rate * (step_value + decay_rate * master)
    shard_weight = new_master.astype(jnp.bfloat16)
    new_weight = in_order(spread(shard_weight, "depth"), "depth", 0)
    return (queries, token_grad, new_master, new_first, new_second, new_weight)


MESH = pl.DeviceIdType.MESH
WIDE = 512
STATE_PARTS = 8
SEND_PARTS = 8
VMEM_LIMIT = 41_000_000


def flip(index, step):
    for bit in range(step.bit_length()):
        if step >> bit & 1:
            index = index + (1 << bit) - 2 * (1 << bit) * (index // (1 << bit) % 2)
    return index


def relay_of(step):
    low = step & -step
    return step - low, low


def fused(
    rows,
    depths,
    grad_scale,
    counts,
    tokens_hbm,
    weight_hbm,
    cotangent_hbm,
    master_hbm,
    first_hbm,
    second_hbm,
    query,
    token_grad,
    product,
    first,
    second,
    pool,
    weight,
    early,
    line,
    slabs,
    turned,
    partial,
    running,
    split,
    inbound,
    piece,
    landed,
    masters,
    local_sem,
    send_sem,
    recv_sem,
    ready_sem,
):
    row, col, depth = lax.axis_index("row"), lax.axis_index("col"), lax.axis_index("depth")
    other = 1 - col
    block, width = line.shape[1], line.shape[2]
    half = block // 2
    features = width // 2
    out_width = weight.shape[1]
    owned = product.shape[0]
    per_col = rows // 2
    singles = [1 << bit for bit in range(depths.bit_length() - 1)]
    composites = [step for step in range(1, depths) if step & (step - 1)]
    stored = sorted({relay_of(step)[0] for step in composites})

    sends = itertools.count()
    shared, spare = {}, []
    locals_ = itertools.count()
    places = itertools.count()
    pending, pooled = [], []

    def slots(count):
        return [next(places) for _ in range(count)][0]

    at_early = slots(per_col)
    at_line = slots(rows)
    at_cross = slots(rows)
    at_cot = slots(rows)
    at_spread = slots(depths * rows)
    at_part = slots(rows)
    at_piece = slots(rows)
    at_final = slots(rows)
    at_run = slots(2 * (rows + 1))
    at_slab = slots(depths)
    at_pair = slots(depths)
    at_weight = slots(depths * SEND_PARTS)

    def where(cond, act):
        if cond is None:
            act()
        else:
            pl.when(cond)(act)

    def both(one, two):
        return two if one is None else jnp.logical_and(one, two)

    def go(
        cond,
        source,
        target,
        place,
        row_to=None,
        col_to=None,
        depth_to=None,
        from_pool=False,
        share=None,
    ):
        peer = (
            row if row_to is None else row_to,
            col if col_to is None else col_to,
            depth if depth_to is None else depth_to,
        )
        if share in shared:
            index = shared[share]
        else:
            index = spare.pop() if spare else next(sends)
        if share is not None:
            shared[share] = index
        copy = pltpu.make_async_remote_copy(
            src_ref=source,
            dst_ref=target,
            send_sem=send_sem.at[index],
            recv_sem=recv_sem.at[place],
            device_id=peer,
            device_id_type=MESH,
        )
        where(cond, copy.start)
        (pooled if from_pool else pending).append((cond, copy.wait_send, index))

    def arrived(cond, target, place):
        copy = pltpu.make_async_remote_copy(
            src_ref=target,
            dst_ref=target,
            send_sem=send_sem.at[0],
            recv_sem=recv_sem.at[place],
            device_id=(row, other, depth),
            device_id_type=MESH,
        )
        where(cond, copy.wait_recv)

    def load(cond, source, target):
        copy = pltpu.make_async_copy(source, target, local_sem.at[next(locals_)])
        where(cond, copy.start)
        return cond, copy.wait

    def cot_rows(step, at, count=1):
        start = (step * rows + at) * block
        return pl.ds(pl.multiple_of(start, block), count * block)

    barrier = pltpu.get_barrier_semaphore()
    peers = [((row + step) % rows, col, depth) for step in range(1, rows)]
    peers += [(row, other, depth)]
    peers += [(row, col, flip(depth, step)) for step in range(1, depths)]
    for peer in peers:
        pl.semaphore_signal(barrier, inc=1, device_id=peer, device_id_type=MESH)
    pl.semaphore_wait(barrier, len(peers))

    mine = pl.ds(pl.multiple_of(col * half, half), half)
    theirs = pl.ds(pl.multiple_of(other * half, half), half)
    owner = row // per_col

    def features_of(at):
        return pl.ds(pl.multiple_of(at % per_col * width, width), width)

    near, far = owner == col, owner != col

    def block_at(index):
        return pl.ds(index * width, width)

    for index in range(per_col):
        go(
            None,
            tokens_hbm.at[theirs, block_at(index)],
            early.at[:, block_at(index)],
            at_early + index,
            col_to=other,
        )
    go(
        near,
        tokens_hbm.at[mine, features_of(row)],
        line.at[row, mine],
        at_cross + row,
        col_to=other,
    )
    for index in range(per_col):
        there = col * per_col + index
        go(
            there != row,
            tokens_hbm.at[mine, block_at(index)],
            line.at[row, mine],
            at_line + row,
            row_to=there,
        )
    right, left = row + 1 < rows, row >= 1
    go(right, cotangent_hbm, pool.at[cot_rows(0, row)], at_cot + row, row_to=row + 1)
    go(left, cotangent_hbm, pool.at[cot_rows(0, row)], at_cot + row, row_to=row - 1)
    for step in reversed(singles):
        go(
            None,
            cotangent_hbm,
            pool.at[cot_rows(step, row)],
            at_spread + step * rows + row,
            depth_to=flip(depth, step),
        )
    weight_here = load(None, weight_hbm, weight)
    cot_here = load(None, cotangent_hbm, pool.at[cot_rows(0, row)])
    own_tokens = [load(near, tokens_hbm.at[mine, features_of(row)], line.at[row, mine])]
    moments = [load(None, first_hbm, first), load(None, second_hbm, second)]
    part_rows = owned // STATE_PARTS
    master_sems = [next(locals_) for _ in range(2)]

    def master_in(part):
        return pltpu.make_async_copy(
            master_hbm.at[pl.ds(part * part_rows, part_rows)],
            masters.at[part % 2],
            local_sem.at[master_sems[part % 2]],
        )

    for part in range(2):
        master_in(part).start()

    for index in range(per_col):
        there = other * per_col + index
        arrived(None, early.at[:, block_at(index)], at_early + index)
        go(
            there != row,
            early.at[:, block_at(index)],
            line.at[row, mine],
            at_line + row,
            row_to=there,
        )
        go(
            there == row,
            early.at[:, block_at(index)],
            line.at[row, mine],
            at_cross + row,
            col_to=other,
        )
    own_tokens.append(load(far, early.at[:, features_of(row)], line.at[row, mine]))

    tiles = width // min(WIDE, features)
    tile = width // tiles

    def gradient_part(at):
        def tile_of(index, carry):
            start = pl.multiple_of(index * tile, tile)
            side = start // features
            value = lax.dot_general(
                pool[cot_rows(0, at)],
                weight[pl.ds(start, tile)],
                (((1,), (1,)), ((), ())),
                preferred_element_type=jnp.float32,
            )
            inside = pl.ds(pl.multiple_of(start % features, tile), tile)
            split[side, at, :, inside] = value
            return carry

        lax.fori_loop(0, tiles, tile_of, 0)

    def send_part(cond, at):
        go(cond, split.at[other, at], inbound.at[at], at_part + at, col_to=other)


    def spread_on(cond, at):
        for step in composites:
            have, low = relay_of(step)
            if step - have == 1:
                arrived(cond, pool.at[cot_rows(have, at)], at_spread + have * rows + at)
            go(
                cond,
                pool.at[cot_rows(have, at)],
                pool.at[cot_rows(step, at)],
                at_spread + step * rows + at,
                depth_to=flip(depth, low),
                from_pool=True,
            )

    def sides_of(step):
        return [(row - step, row >= step), (row + step, row + step < rows)][: 2 if step else 1]

    def tokens_in(step, which):
        for side, (at, cond) in enumerate(sides_of(step)):
            cond = both(cond, which)
            arrived(cond, line.at[at, mine], at_line + at)
            go(
                cond,
                line.at[at, mine],
                line.at[at, mine],
                at_cross + at,
                col_to=other,
                share=("tokens", step, side),
            )

    def crossed(which, step):
        for at, cond in sides_of(step):
            arrived(both(cond, which), line.at[at, theirs], at_cross + at)

    def slabs_out(which, tokens, place):
        for step in reversed(range(2, depths)):
            if place == at_pair and step in composites:
                continue
            there = flip(depth, step)
            go(
                which,
                line.at[:, tokens, pl.ds(pl.multiple_of(there * owned, owned), owned)],
                slabs.at[step - 1, :, tokens],
                place + step,
                depth_to=there,
                share=("slab", step, place),
            )

    def slabs_across(which):
        for step in composites:
            slab = slabs.at[step - 1, :, mine]
            arrived(which, slab, at_slab + step)
            go(which, slab, slab, at_pair + step, col_to=other, share=("across", step))

    def cots_in(step):
        onward = [(row + 1 < rows, row + 1), (row >= 1, row - 1)]
        for (at, cond), (more, there) in zip(sides_of(step), onward):
            arrived(cond, pool.at[cot_rows(0, at)], at_cot + at)
            go(
                both(cond, more),
                pool.at[cot_rows(0, at)],
                pool.at[cot_rows(0, at)],
                at_cot + at,
                row_to=there,
                from_pool=True,
            )
            for single in reversed(singles):
                go(
                    cond,
                    pool.at[cot_rows(0, at)],
                    pool.at[cot_rows(single, at)],
                    at_spread + single * rows + at,
                    depth_to=flip(depth, single),
                    from_pool=True,
                )

    def on_sides(step, act, extra=None):
        def one_side(index, carry):
            at = row + step * (2 * index - 1)

            @pl.when(both(extra, jnp.logical_and(at >= 0, at < rows)))
            def _():
                act(at)

            return carry

        lax.fori_loop(0, 2 if step else 1, one_side, 0)

    def parts_make(step):
        on_sides(step, gradient_part)

    def parts_out(step, which=None):
        for at, cond in sides_of(step):
            send_part(both(which, cond), at)

    def spread_step(step):
        for at, cond in sides_of(step):
            spread_on(cond, at)

    def pieces_home(step, which=None):
        for at, cond in sides_of(step):
            arrived(both(which, cond), inbound.at[at], at_part + at)
        on_sides(step, finish_piece, which)
        if step:
            for side, (at, cond) in enumerate(sides_of(step)):
                return_piece(both(which, cond), at, ("piece", step, side))

    at_end = jnp.logical_or(row == 0, row == rows - 1)
    inside = jnp.logical_and(row > 0, row < rows - 1)

    def run_begin(part, which, step, held=False):
        inner = both(which, at_end)
        side = jnp.where(part == 0, owner, 1 - owner)
        on_sides(step, lambda at: query_part(at, side), inner)
        if not held:
            run_out(part, which, step)

    def run_out(part, which, step):
        share = (f"begin{part}", step)
        run_right(both(which, row == 0), row + step, part, share)
        run_left(both(which, row == rows - 1), row - step, 1 - part, share)

    query_tiles = out_width // min(WIDE, out_width)
    query_tile = out_width // query_tiles

    def half_of(side):
        return pl.ds(pl.multiple_of(side * half, half), half)

    def query_part(at, side):
        def tile_of(index, carry):
            across = pl.ds(pl.multiple_of(index * query_tile, query_tile), query_tile)
            partial[at, half_of(side), across] = jnp.dot(
                line[at, half_of(side)], weight[:, across], preferred_element_type=jnp.float32
            )
            return carry

        lax.fori_loop(0, query_tiles, tile_of, 0)

    def run_place(slot, side):
        return at_run + side * (rows + 1) + slot

    def run_right(cond, at, side, share):
        go(
            cond,
            partial.at[at, half_of(side)],
            running.at[at + 1, half_of(side)],
            run_place(at + 1, side),
            row_to=row + 1,
            share=share,
        )

    def run_left(cond, at, side, share):
        go(
            cond,
            partial.at[at, half_of(side)],
            running.at[at, half_of(side)],
            run_place(at, side),
            row_to=row - 1,
            share=share,
        )

    def run_here(cond, slot, side):
        arrived(cond, running.at[slot, half_of(side)], run_place(slot, side))

    def add_running(at, slot, side):
        def rows_of(index, carry):
            down = pl.ds(pl.multiple_of(side * half + index * 16, 16), 16)
            partial[at, down] = partial[at, down] + running[slot, down]
            return carry

        lax.fori_loop(0, half // 16, rows_of, 0)

    def finish_piece(at):
        def rows_of(index, carry):
            down = pl.ds(pl.multiple_of(index * 16, 16), 16)
            value = split[col, at, down] + inbound[at, down]
            piece[at, down] = value.astype(piece.dtype)
            return carry

        lax.fori_loop(0, block // 16, rows_of, 0)

    def columns_of(source, side):
        start = source % per_col * width + side * features
        return pl.ds(pl.multiple_of(start, features), features)

    def return_piece(cond, at, share):
        go(
            both(cond, owner == col),
            piece.at[at],
            token_grad.at[:, columns_of(row, col)],
            at_piece + row,
            row_to=at,
            share=share,
        )
        go(
            both(cond, owner != col),
            piece.at[at],
            landed.at[row],
            at_piece + row,
            row_to=at,
            share=share,
        )

    product_tiles = out_width // min(WIDE, out_width)
    product_tile = out_width // product_tiles

    def gradient(step, start=0, count=rows):
        across = pl.ds(pl.multiple_of(depth * owned, owned), owned)
        taken = pl.ds(start, count)
        slab = slabs[step - 1, taken] if step else line[taken, :, across]
        deep = pl.ds(0, count * block)
        turned[:, deep] = slab.reshape(count * block, owned).T

        def tile_of(index, carry):
            across = pl.ds(pl.multiple_of(index * product_tile, product_tile), product_tile)
            value = jnp.dot(
                turned[:, deep],
                pool[cot_rows(step, start, count), across],
                preferred_element_type=jnp.float32,
            )
            product[:, across] = value + product[:, across] if step else value
            return carry

        lax.fori_loop(0, product_tiles, tile_of, 0)

    last = jnp.where(row < per_col, rows - 1, 0)
    before_last = jnp.where(row < per_col, 0, 1)

    def wait_slab(step):
        if step == 1:
            arrived(None, slabs.at[step - 1], at_slab + step)
        else:
            if step not in composites:
                arrived(None, slabs.at[step - 1, :, mine], at_slab + step)
            arrived(None, slabs.at[step - 1, :, theirs], at_pair + step)

    def wait_spread(step, which):
        if step not in stored:
            for at in range(rows):
                cond = None if which is None else (at == last if which else at != last)
                arrived(cond, pool.at[cot_rows(step, at)], at_spread + step * rows + at)

    def wait_whole(step):
        wait_slab(step)
        wait_spread(step, None)

    def gradient_most(step):
        wait_slab(step)
        wait_spread(step, False)
        gradient(step, before_last, rows - 1)

    def gradient_last(step):
        wait_spread(step, True)
        gradient(step, last, 1)

    def run_step(step, part, origin, which=None):
        for cond, at, slot, onward, side, begun in (
            (row > 0, row + step, row + step + 1, run_right, part, col == origin),
            (row < rows - 1, row - step, row - step, run_left, 1 - part, col != origin),
        ):
            cond = both(which, both(begun, both(cond, jnp.logical_and(at >= 0, at < rows))))
            run_here(cond, slot, side)

            def add(at=at, slot=slot, side=side):
                add_running(at, slot, side)

            where(cond, add)
            onward(cond, at, side, ("run", step, part, origin, which is near))

    def wait_first():
        weight_here[1]()
        cot_here[1]()

    def wait_own(which):
        cond, wait = own_tokens[0 if which is near else 1]
        where(cond, wait)

    def inner_queries(part):
        side = owner if part == 0 else 1 - owner
        for step in reversed(range(1, rows)):
            on_sides(step, lambda at: query_part(at, side), inside)
        query_part(row, side)

    wait_first()
    parts_make(0)
    spread_step(0)
    for step in range(1, rows):
        tokens_in(step, near)
    wait_own(near)
    slabs_out(near, mine, at_slab)
    parts_out(0, far)
    for step in reversed(range(1, rows)):
        run_begin(0, near, step)
    cots_in(1)
    for step in range(1, rows):
        tokens_in(step, far)
        crossed(far, step)
        run_begin(0, far, step)
    wait_own(far)
    crossed(far, 0)
    slabs_out(far, mine, at_slab)
    slabs_out(far, theirs, at_pair)
    for step in reversed(range(1, rows)):
        run_begin(1, far, step, step < rows - 1)
    inner_queries(0)
    for step in reversed(range(2, rows)):
        run_step(step, 0, 0, near)
    parts_make(1)
    settled = len(pending)
    parts_out(1)
    slabs_across(near)
    cots_in(2)
    run_step(1, 0, 1, far)
    run_step(1, 0, 0, near)
    for step in reversed(range(rows)):
        crossed(near, step)
        if step:
            run_begin(1, near, step, step < rows - 1)
    slabs_out(near, theirs, at_pair)
    there = flip(depth, 1)
    across = pl.ds(pl.multiple_of(there * owned, owned), owned)
    go(None, line.at[:, :, across], slabs.at[0], at_slab + 1, depth_to=there)
    inner_queries(1)

    def near_depths():
        gradient(0)
        wait_whole(1)
        gradient(1)

    where(inside, near_depths)
    for step in range(2, rows):
        run_step(step, 0, 1, far)
    run_step(1, 0, 0, far)
    slabs_across(far)
    parts_make(2)
    parts_out(2)
    spread_step(1)
    for step in range(3, rows):
        cots_in(step)
        parts_make(step)
        parts_out(step)
    parts_out(0, near)
    where(at_end, near_depths)
    for step in range(2, rows - 1):
        spread_step(step)
    early_pieces = jnp.logical_or(near, at_end)
    pieces_home(1, early_pieces)
    for step in reversed(range(2, rows)):
        run_step(step, 1, 0)
        run_step(step, 1, 1)
    run_step(1, 0, 1, near)
    for step in range(2, depths):
        gradient_most(step)
    pieces_home(2, at_end)
    spread_step(rows - 1)
    for step in range(2, depths):
        gradient_last(step)

    slow = {index for key, index in shared.items() if key[0] == "begin1"}
    done = [entry for entry in pending[:settled] if entry[2] not in slow]
    pending[:settled] = [entry for entry in pending[:settled] if entry[2] in slow]
    for cond, wait, index in pooled + done:
        where(cond, wait)
        if index not in shared.values():
            spare.append(index)
    spare.extend({index for key, index in shared.items() if key[0] in ("tokens", "begin0")})
    for index, single in enumerate(singles):
        pl.semaphore_signal(
            ready_sem.at[index],
            inc=1,
            device_id=(row, col, flip(depth, single)),
            device_id_type=MESH,
        )
    for _, wait in moments:
        wait()

    send_rows = owned // SEND_PARTS

    def weight_rows(at, part):
        start = at * owned + part * send_rows
        return pl.ds(pl.multiple_of(start, send_rows), send_rows)

    def optimize(part):
        master_in(part).wait()

        def rows_of(index, carry):
            down = pl.ds(pl.multiple_of(index * 16, 16), 16)
            whole = pl.ds(pl.multiple_of(part * part_rows + index * 16, 16), 16)
            kept = pl.ds(pl.multiple_of(depth * owned + part * part_rows + index * 16, 16), 16)
            grad = product[whole] * grad_scale
            new_first = beta_one * first[whole] + (1.0 - beta_one) * grad
            new_second = beta_two * second[whole] + (1.0 - beta_two) * grad * grad
            step_value = new_first / bias_one / (jnp.sqrt(new_second / bias_two) + adam_eps)
            old = masters[part % 2, down]
            new_master = old - learn_rate * (step_value + decay_rate * old)
            product[whole] = new_master
            first[whole] = new_first
            second[whole] = new_second
            pool[kept] = new_master.astype(pool.dtype)
            return carry

        lax.fori_loop(0, part_rows // 16, rows_of, 0)
        if part + 2 < STATE_PARTS:
            master_in(part + 2).start()
        if (part + 1) % (STATE_PARTS // SEND_PARTS):
            return
        sent = part // (STATE_PARTS // SEND_PARTS)
        source = pool.at[weight_rows(depth, sent)]
        for index, single in reversed(list(enumerate(singles))):
            if sent == 0:
                pl.semaphore_wait(ready_sem.at[index], 1)
            go(
                None,
                source,
                source,
                at_weight + single * SEND_PARTS + sent,
                depth_to=flip(depth, single),
            )

    for part in range(STATE_PARTS):
        optimize(part)
    pieces_home(1, jnp.logical_not(early_pieces))
    pieces_home(2, inside)
    for step in range(3, rows):
        pieces_home(step)
    for step in reversed(range(1, rows - 1)):
        run_out(1, None, step)
    run_step(1, 1, 1, near)
    pieces_home(0)
    own_piece = load(near, piece.at[row], token_grad.at[:, columns_of(row, col)])
    go(
        far,
        piece.at[row],
        token_grad.at[:, columns_of(row, col)],
        at_final + row,
        col_to=other,
    )
    for step in range(1, rows):
        for at, cond in ((row - step, row >= step), (row + step, row + step < rows)):
            across = at // per_col != col
            arrived(both(cond, across), landed.at[at], at_piece + at)
            go(
                both(cond, across),
                landed.at[at],
                token_grad.at[:, columns_of(at, col)],
                at_final + at,
                col_to=other,
            )

    run_step(1, 1, 0, far)
    run_step(1, 1, 0, near)
    run_step(1, 1, 1, far)

    for sent in range(SEND_PARTS):
        for step in composites:
            have, low = relay_of(step)
            source = pool.at[weight_rows(flip(depth, have), sent)]
            if step - have == 1:
                arrived(None, source, at_weight + have * SEND_PARTS + sent)
            go(
                None,
                source,
                source,
                at_weight + step * SEND_PARTS + sent,
                depth_to=flip(depth, low),
            )

    from_left, from_right = row > 0, row < rows - 1
    for side in range(2):
        for cond, slot in ((from_left, row + 1), (from_right, row)):
            run_here(cond, slot, side)

            def add(slot=slot, side=side):
                add_running(row, slot, side)

            where(cond, add)

    def rounded(index, carry):
        down = pl.ds(pl.multiple_of(index * 16, 16), 16)
        query[down] = partial[row, down].astype(query.dtype)
        return carry

    lax.fori_loop(0, block // 16, rounded, 0)

    for at in range(rows):
        away = jnp.logical_and(at != row, at // per_col == col)
        arrived(away, token_grad.at[:, columns_of(at, col)], at_piece + at)
        arrived(at // per_col == col, token_grad.at[:, columns_of(at, other)], at_final + at)
    for sent in range(SEND_PARTS):
        for step in range(1, depths):
            if step not in stored:
                place = at_weight + step * SEND_PARTS + sent
                arrived(None, pool.at[weight_rows(flip(depth, step), sent)], place)
    counts.append((next(locals_), next(sends), next(places)))
    where(*own_piece)
    for cond, wait, _ in pending:
        where(cond, wait)


def write_out(*refs):
    held, outs, sem = refs[:6], refs[6:12], refs[12]
    copies = []
    for index, (source, target) in enumerate(zip(held, outs)):
        copies.append(
            pltpu.make_async_copy(
                source.at[pl.ds(0, target.shape[0])], target, sem.at[index]
            )
        )
    for copy in copies:
        copy.start()
    for copy in copies:
        copy.wait()


def step(mesh, tokens, weight, cotangent, master, first_moment, second_moment):
    rows, cols, depths = (mesh.shape[name] for name in ("row", "col", "depth"))
    block, width = tokens.shape[0], weight.shape[0]
    out_width, owned = weight.shape[1], master.shape[0]
    fits = (
        cols == 2
        and rows > 2
        and rows % 2 == 0
        and depths > 2
        and depths & (depths - 1) == 0
        and block % 32 == 0
        and width % 256 == 0
        and out_width % 128 == 0
        and owned % (16 * STATE_PARTS) == 0
    )
    if not fits:
        return plain(tokens, weight, cotangent, master, first_moment, second_moment)
    small, wide = jnp.bfloat16, jnp.float32
    pool_rows = max(depths * rows * block, width)
    shapes = [
        ((width, out_width), small),
        ((block // 2, tokens.shape[1]), small),
        ((rows, block, width), small),
        ((depths - 1, rows, block, owned), small),
        ((owned, rows * block), small),
        ((rows, block, out_width), wide),
        ((rows + 1, block, out_width), wide),
        ((2, rows, block, width // 2), wide),
        ((rows, block, width // 2), wide),
        ((rows, block, width // 2), small),
        ((rows, block, width // 2), small),
        ((2, owned // STATE_PARTS, out_width), wide),
    ]
    total_tokens = block * rows * depths
    outs = [
        ((block, out_width), small),
        (tokens.shape, small),
        (master.shape, wide),
        (master.shape, wide),
        (master.shape, wide),
        ((pool_rows, out_width), small),
    ]

    def moved(counts, *semaphores):
        return pl.pallas_call(
            functools.partial(fused, rows, depths, 1.0 / math.sqrt(total_tokens), counts),
            out_shape=[pltpu.VMEM(shape, dtype) for shape, dtype in outs],
            in_specs=[pl.BlockSpec(memory_space=pl.ANY)] * 6,
            out_specs=[pl.BlockSpec(memory_space=pltpu.VMEM)] * 6,
            scratch_shapes=[pltpu.VMEM(shape, dtype) for shape, dtype in shapes]
            + [pltpu.SemaphoreType.DMA((count,)) for count in semaphores]
            + [pltpu.SemaphoreType.REGULAR((depths.bit_length() - 1,))],
            compiler_params=pltpu.CompilerParams(
                collective_id=0, has_side_effects=True, vmem_limit_bytes=VMEM_LIMIT
            ),
        )

    arrays = (tokens, weight, cotangent, master, first_moment, second_moment)
    counts = []
    jax.eval_shape(moved(counts, 512, 512, 512), *arrays)
    held = moved([], *counts[0])(*arrays)
    outs[-1] = (weight.shape, small)
    return pl.pallas_call(
        write_out,
        out_shape=[jax.ShapeDtypeStruct(shape, dtype) for shape, dtype in outs],
        in_specs=[pl.BlockSpec(memory_space=pltpu.VMEM)] * 6,
        out_specs=[pl.BlockSpec(memory_space=pl.ANY)] * 6,
        scratch_shapes=[pltpu.SemaphoreType.DMA((6,))],
        compiler_params=pltpu.CompilerParams(vmem_limit_bytes=1 << 20),
    )(*(pltpu.with_memory_space_constraint(value, pltpu.VMEM) for value in held))


def solution(mesh):
    in_specs = (
        P(("row", "depth"), "col"),
        P("row", "col"),
        P(("row", "depth"), "col"),
        P(("row", "depth"), "col"),
        P(("row", "depth"), "col"),
        P(("row", "depth"), "col"),
    )
    out_specs = (
        P(("row", "depth"), "col"),
        P(("row", "depth"), "col"),
        P(("row", "depth"), "col"),
        P(("row", "depth"), "col"),
        P(("row", "depth"), "col"),
        P("row", "col"),
    )
    return jax.shard_map(functools.partial(step, mesh), mesh=mesh, in_specs=in_specs, out_specs=out_specs, check_vma=False)
```

```python
import functools
import itertools
import math

import jax
import jax.numpy as jnp
from jax import lax
from jax.experimental import pallas as pl
from jax.experimental.pallas import tpu as pltpu
from jax.sharding import PartitionSpec as P

beta_one = 0.9
beta_two = 0.95
learn_rate = 0.02
decay_rate = 0.1
adam_eps = 1e-08
bias_one = 1.0 - 0.9**50
bias_two = 1.0 - 0.95**50


def swap(value, axis, step):
    size = lax.axis_size(axis)
    return lax.ppermute(value, axis, [(i, i ^ step) for i in range(size)])


def spread(value, axis):
    pieces = [value]
    for step in range(1, lax.axis_size(axis)):
        top = 1 << (step.bit_length() - 1)
        low = step & -step
        pieces.append(swap(pieces[step - low], axis, low) if step != top else swap(value, axis, step))
    return pieces


def in_order(pieces, axis, dim):
    me = lax.axis_index(axis)
    size = pieces[0].shape[dim]
    shape = list(pieces[0].shape)
    shape[dim] = size * len(pieces)
    whole = jnp.zeros(shape, pieces[0].dtype)
    for step, piece in enumerate(pieces):
        whole = lax.dynamic_update_slice_in_dim(whole, piece, (me ^ step) * size, dim)
    return whole


def plain(tokens, weight, cotangent, master, first_moment, second_moment):
    rows, cols, depths = lax.axis_size("row"), lax.axis_size("col"), lax.axis_size("depth")
    col_at, depth_at = lax.axis_index("col"), lax.axis_index("depth")
    block = tokens.shape[0]
    total_tokens = block * rows * depths
    grad_scale = 1.0 / math.sqrt(total_tokens)
    full_rows = in_order(spread(tokens, "col"), "col", 1)
    line_cotangent = lax.all_gather(cotangent, "row", axis=0, tiled=True)
    line_tokens = lax.all_to_all(full_rows, "row", split_axis=1, concat_axis=0, tiled=True)
    features = weight.shape[0] // cols
    parts = []
    for step in reversed(range(cols)):
        panel = lax.dynamic_slice_in_dim(weight, (col_at ^ step) * features, features, 0)
        part = lax.dot_general(
            line_cotangent, panel, (((1,), (1,)), ((), ())), preferred_element_type=jnp.float32
        )
        parts.append(swap(part, "col", step) if step else part)
    piece = sum(parts[1:], parts[0]).astype(jnp.bfloat16)
    partial_queries = jnp.dot(line_tokens, weight, preferred_element_type=jnp.float32)
    queries = lax.psum_scatter(partial_queries, "row", scatter_dimension=0, tiled=True).astype(
        jnp.bfloat16
    )
    piece = lax.all_to_all(
        piece.reshape(rows, block, -1), "row", split_axis=0, concat_axis=0, tiled=True
    )
    piece = lax.all_to_all(
        piece.reshape(cols, rows // cols, block, -1), "col", split_axis=0, concat_axis=0, tiled=True
    )
    token_grad = piece.transpose(2, 1, 0, 3).reshape(tokens.shape)
    shard = line_tokens.shape[1] // depths
    product = 0.0
    for step, other_cotangent in enumerate(spread(line_cotangent, "depth")):
        slab = lax.dynamic_slice_in_dim(line_tokens, (depth_at ^ step) * shard, shard, 1)
        slab = swap(slab, "depth", step) if step else slab
        product = product + lax.dot_general(
            slab, other_cotangent, (((0,), (0,)), ((), ())), preferred_element_type=jnp.float32
        )
    grad = product * grad_scale
    new_first = beta_one * first_moment + (1.0 - beta_one) * grad
    new_second = beta_two * second_moment + (1.0 - beta_two) * grad * grad
    step_value = new_first / bias_one / (jnp.sqrt(new_second / bias_two) + adam_eps)
    new_master = master - learn_rate * (step_value + decay_rate * master)
    shard_weight = new_master.astype(jnp.bfloat16)
    new_weight = in_order(spread(shard_weight, "depth"), "depth", 0)
    return (queries, token_grad, new_master, new_first, new_second, new_weight)


MESH = pl.DeviceIdType.MESH
WIDE = 1024
STATE_PARTS = 8
SEND_PARTS = 8
VMEM_LIMIT = 41_000_000
VMEM_BYTES = 64 << 20


def flip(index, step):
    for bit in range(step.bit_length()):
        if step >> bit & 1:
            index = index + (1 << bit) - 2 * (1 << bit) * (index // (1 << bit) % 2)
    return index


def relay_of(step):
    low = step & -step
    return step - low, low


def fused(
    rows,
    depths,
    grad_scale,
    counts,
    tokens_hbm,
    weight_hbm,
    cotangent_hbm,
    master_hbm,
    first_hbm,
    second_hbm,
    query,
    token_grad,
    product,
    first,
    second,
    pool,
    weight,
    early,
    line,
    slabs,
    turned,
    partial,
    running,
    split,
    inbound,
    piece,
    landed,
    masters,
    local_sem,
    send_sem,
    recv_sem,
    ready_sem,
):
    row, col, depth = lax.axis_index("row"), lax.axis_index("col"), lax.axis_index("depth")
    other = 1 - col
    block, width = line.shape[1], line.shape[2]
    half = block // 2
    features = width // 2
    out_width = weight.shape[1]
    owned = product.shape[0]
    per_col = rows // 2
    singles = [1 << bit for bit in range(depths.bit_length() - 1)]
    composites = [step for step in range(1, depths) if step & (step - 1)]
    stored = sorted({relay_of(step)[0] for step in composites})

    sends = itertools.count()
    shared, spare = {}, []
    locals_ = itertools.count()
    places = itertools.count()
    pending, pooled = [], []

    def slots(count):
        return [next(places) for _ in range(count)][0]

    at_early = slots(per_col)
    at_line = slots(rows)
    at_cross = slots(rows)
    at_cot = slots(rows)
    at_spread = slots(depths * rows)
    at_part = slots(rows)
    at_piece = slots(rows)
    at_final = slots(rows)
    at_run = slots(2 * (rows + 1))
    at_slab = slots(depths)
    at_pair = slots(depths)
    at_weight = slots(depths * SEND_PARTS)

    def where(cond, act):
        if cond is None:
            act()
        else:
            pl.when(cond)(act)

    def both(one, two):
        return two if one is None else jnp.logical_and(one, two)

    def go(
        cond,
        source,
        target,
        place,
        row_to=None,
        col_to=None,
        depth_to=None,
        from_pool=False,
        share=None,
    ):
        peer = (
            row if row_to is None else row_to,
            col if col_to is None else col_to,
            depth if depth_to is None else depth_to,
        )
        if share in shared:
            index = shared[share]
        else:
            index = spare.pop() if spare else next(sends)
        if share is not None:
            shared[share] = index
        copy = pltpu.make_async_remote_copy(
            src_ref=source,
            dst_ref=target,
            send_sem=send_sem.at[index],
            recv_sem=recv_sem.at[place],
            device_id=peer,
            device_id_type=MESH,
        )
        where(cond, copy.start)
        (pooled if from_pool else pending).append((cond, copy.wait_send, index))

    def arrived(cond, target, place):
        copy = pltpu.make_async_remote_copy(
            src_ref=target,
            dst_ref=target,
            send_sem=send_sem.at[0],
            recv_sem=recv_sem.at[place],
            device_id=(row, other, depth),
            device_id_type=MESH,
        )
        where(cond, copy.wait_recv)

    def load(cond, source, target):
        copy = pltpu.make_async_copy(source, target, local_sem.at[next(locals_)])
        where(cond, copy.start)
        return cond, copy.wait

    def cot_rows(step, at, count=1):
        start = (step * rows + at) * block
        return pl.ds(pl.multiple_of(start, block), count * block)

    barrier = pltpu.get_barrier_semaphore()
    peers = [((row + step) % rows, col, depth) for step in range(1, rows)]
    peers += [(row, other, depth)]
    peers += [(row, col, flip(depth, step)) for step in range(1, depths)]
    for peer in peers:
        pl.semaphore_signal(barrier, inc=1, device_id=peer, device_id_type=MESH)
    pl.semaphore_wait(barrier, len(peers))

    mine = pl.ds(pl.multiple_of(col * half, half), half)
    theirs = pl.ds(pl.multiple_of(other * half, half), half)
    owner = row // per_col

    def features_of(at):
        return pl.ds(pl.multiple_of(at % per_col * width, width), width)

    near, far = owner == col, owner != col

    def block_at(index):
        return pl.ds(index * width, width)

    for index in range(per_col):
        go(
            None,
            tokens_hbm.at[theirs, block_at(index)],
            early.at[:, block_at(index)],
            at_early + index,
            col_to=other,
        )
    go(
        near,
        tokens_hbm.at[mine, features_of(row)],
        line.at[row, mine],
        at_cross + row,
        col_to=other,
    )
    for index in range(per_col):
        there = col * per_col + index
        go(
            there != row,
            tokens_hbm.at[mine, block_at(index)],
            line.at[row, mine],
            at_line + row,
            row_to=there,
        )
    right, left = row + 1 < rows, row >= 1
    go(right, cotangent_hbm, pool.at[cot_rows(0, row)], at_cot + row, row_to=row + 1)
    go(left, cotangent_hbm, pool.at[cot_rows(0, row)], at_cot + row, row_to=row - 1)
    for step in reversed(singles):
        go(
            None,
            cotangent_hbm,
            pool.at[cot_rows(step, row)],
            at_spread + step * rows + row,
            depth_to=flip(depth, step),
        )
    weight_here = load(None, weight_hbm, weight)
    cot_here = load(None, cotangent_hbm, pool.at[cot_rows(0, row)])
    own_tokens = [load(near, tokens_hbm.at[mine, features_of(row)], line.at[row, mine])]
    moments = [load(None, first_hbm, first), load(None, second_hbm, second)]
    part_rows = owned // STATE_PARTS
    master_sems = [next(locals_) for _ in range(2)]

    def master_in(part):
        return pltpu.make_async_copy(
            master_hbm.at[pl.ds(part * part_rows, part_rows)],
            masters.at[part % 2],
            local_sem.at[master_sems[part % 2]],
        )

    for part in range(2):
        master_in(part).start()

    for index in range(per_col):
        there = other * per_col + index
        arrived(None, early.at[:, block_at(index)], at_early + index)
        go(
            there != row,
            early.at[:, block_at(index)],
            line.at[row, mine],
            at_line + row,
            row_to=there,
        )
        go(
            there == row,
            early.at[:, block_at(index)],
            line.at[row, mine],
            at_cross + row,
            col_to=other,
        )
    own_tokens.append(load(far, early.at[:, features_of(row)], line.at[row, mine]))

    tiles = width // min(WIDE, features)
    tile = width // tiles

    def gradient_part(at):
        def tile_of(index, carry):
            start = pl.multiple_of(index * tile, tile)
            side = start // features
            value = lax.dot_general(
                pool[cot_rows(0, at)],
                weight[pl.ds(start, tile)],
                (((1,), (1,)), ((), ())),
                preferred_element_type=jnp.float32,
            )
            inside = pl.ds(pl.multiple_of(start % features, tile), tile)
            split[side, at, :, inside] = value
            return carry

        lax.fori_loop(0, tiles, tile_of, 0)

    def send_part(cond, at):
        go(cond, split.at[other, at], inbound.at[at], at_part + at, col_to=other)


    def spread_on(cond, at):
        for step in composites:
            have, low = relay_of(step)
            if step - have == 1:
                arrived(cond, pool.at[cot_rows(have, at)], at_spread + have * rows + at)
            go(
                cond,
                pool.at[cot_rows(have, at)],
                pool.at[cot_rows(step, at)],
                at_spread + step * rows + at,
                depth_to=flip(depth, low),
                from_pool=True,
            )

    def sides_of(step):
        return [(row - step, row >= step), (row + step, row + step < rows)][: 2 if step else 1]

    def tokens_in(step, which):
        for side, (at, cond) in enumerate(sides_of(step)):
            cond = both(cond, which)
            arrived(cond, line.at[at, mine], at_line + at)
            go(
                cond,
                line.at[at, mine],
                line.at[at, mine],
                at_cross + at,
                col_to=other,
                share=("tokens", step, side),
            )

    def crossed(which, step):
        for at, cond in sides_of(step):
            arrived(both(cond, which), line.at[at, theirs], at_cross + at)

    def slabs_out(which, tokens, place):
        for step in reversed(range(2, depths)):
            if place == at_pair and step in composites:
                continue
            there = flip(depth, step)
            go(
                which,
                line.at[:, tokens, pl.ds(pl.multiple_of(there * owned, owned), owned)],
                slabs.at[step - 1, :, tokens],
                place + step,
                depth_to=there,
                share=("slab", step, place),
            )

    def slabs_across(which):
        for step in composites:
            slab = slabs.at[step - 1, :, mine]
            arrived(which, slab, at_slab + step)
            go(which, slab, slab, at_pair + step, col_to=other, share=("across", step))

    def cots_in(step):
        onward = [(row + 1 < rows, row + 1), (row >= 1, row - 1)]
        for (at, cond), (more, there) in zip(sides_of(step), onward):
            arrived(cond, pool.at[cot_rows(0, at)], at_cot + at)
            go(
                both(cond, more),
                pool.at[cot_rows(0, at)],
                pool.at[cot_rows(0, at)],
                at_cot + at,
                row_to=there,
                from_pool=True,
            )
            for single in reversed(singles):
                go(
                    cond,
                    pool.at[cot_rows(0, at)],
                    pool.at[cot_rows(single, at)],
                    at_spread + single * rows + at,
                    depth_to=flip(depth, single),
                    from_pool=True,
                )

    def on_sides(step, act, extra=None):
        def one_side(index, carry):
            at = row + step * (2 * index - 1)

            @pl.when(both(extra, jnp.logical_and(at >= 0, at < rows)))
            def _():
                act(at)

            return carry

        lax.fori_loop(0, 2 if step else 1, one_side, 0)

    def parts_make(step):
        on_sides(step, gradient_part)

    def parts_out(step, which=None):
        for at, cond in sides_of(step):
            send_part(both(which, cond), at)

    def spread_step(step):
        for at, cond in sides_of(step):
            spread_on(cond, at)

    def pieces_home(step, which=None):
        for at, cond in sides_of(step):
            arrived(both(which, cond), inbound.at[at], at_part + at)
        on_sides(step, finish_piece, which)
        if step:
            for side, (at, cond) in enumerate(sides_of(step)):
                return_piece(both(which, cond), at, ("piece", step, side))

    at_end = jnp.logical_or(row == 0, row == rows - 1)
    inside = jnp.logical_and(row > 0, row < rows - 1)

    def run_begin(part, which, step, held=False):
        inner = both(which, at_end)
        side = jnp.where(part == 0, owner, 1 - owner)
        on_sides(step, lambda at: query_part(at, side), inner)
        if not held:
            run_out(part, which, step)

    def run_out(part, which, step):
        share = (f"begin{part}", step)
        run_right(both(which, row == 0), row + step, part, share)
        run_left(both(which, row == rows - 1), row - step, 1 - part, share)

    query_tiles = out_width // min(WIDE, out_width)
    query_tile = out_width // query_tiles

    def half_of(side):
        return pl.ds(pl.multiple_of(side * half, half), half)

    def query_part(at, side):
        def tile_of(index, carry):
            across = pl.ds(pl.multiple_of(index * query_tile, query_tile), query_tile)
            partial[at, half_of(side), across] = jnp.dot(
                line[at, half_of(side)], weight[:, across], preferred_element_type=jnp.float32
            )
            return carry

        lax.fori_loop(0, query_tiles, tile_of, 0)

    def run_place(slot, side):
        return at_run + side * (rows + 1) + slot

    def run_right(cond, at, side, share):
        go(
            cond,
            partial.at[at, half_of(side)],
            running.at[at + 1, half_of(side)],
            run_place(at + 1, side),
            row_to=row + 1,
            share=share,
        )

    def run_left(cond, at, side, share):
        go(
            cond,
            partial.at[at, half_of(side)],
            running.at[at, half_of(side)],
            run_place(at, side),
            row_to=row - 1,
            share=share,
        )

    def run_here(cond, slot, side):
        arrived(cond, running.at[slot, half_of(side)], run_place(slot, side))

    def add_running(at, slot, side):
        def rows_of(index, carry):
            down = pl.ds(pl.multiple_of(side * half + index * 16, 16), 16)
            partial[at, down] = partial[at, down] + running[slot, down]
            return carry

        lax.fori_loop(0, half // 16, rows_of, 0)

    def finish_piece(at):
        def rows_of(index, carry):
            down = pl.ds(pl.multiple_of(index * 16, 16), 16)
            value = split[col, at, down] + inbound[at, down]
            piece[at, down] = value.astype(piece.dtype)
            return carry

        lax.fori_loop(0, block // 16, rows_of, 0)

    def columns_of(source, side):
        start = source % per_col * width + side * features
        return pl.ds(pl.multiple_of(start, features), features)

    def return_piece(cond, at, share):
        go(
            both(cond, owner == col),
            piece.at[at],
            token_grad.at[:, columns_of(row, col)],
            at_piece + row,
            row_to=at,
            share=share,
        )
        go(
            both(cond, owner != col),
            piece.at[at],
            landed.at[row],
            at_piece + row,
            row_to=at,
            share=share,
        )

    product_tiles = out_width // min(WIDE, out_width)
    product_tile = out_width // product_tiles

    def gradient(step, start=0, count=rows):
        across = pl.ds(pl.multiple_of(depth * owned, owned), owned)
        taken = pl.ds(start, count)
        slab = slabs[step - 1, taken] if step else line[taken, :, across]
        deep = pl.ds(0, count * block)
        turned[:, deep] = slab.reshape(count * block, owned).T

        def tile_of(index, carry):
            across = pl.ds(pl.multiple_of(index * product_tile, product_tile), product_tile)
            value = jnp.dot(
                turned[:, deep],
                pool[cot_rows(step, start, count), across],
                preferred_element_type=jnp.float32,
            )
            product[:, across] = value + product[:, across] if step else value
            return carry

        lax.fori_loop(0, product_tiles, tile_of, 0)

    last = jnp.where(row < per_col, rows - 1, 0)
    before_last = jnp.where(row < per_col, 0, 1)

    def wait_slab(step):
        if step == 1:
            arrived(None, slabs.at[step - 1], at_slab + step)
        else:
            if step not in composites:
                arrived(None, slabs.at[step - 1, :, mine], at_slab + step)
            arrived(None, slabs.at[step - 1, :, theirs], at_pair + step)

    def wait_spread(step, which):
        if step not in stored:
            for at in range(rows):
                cond = None if which is None else (at == last if which else at != last)
                arrived(cond, pool.at[cot_rows(step, at)], at_spread + step * rows + at)

    def wait_whole(step):
        wait_slab(step)
        wait_spread(step, None)

    def gradient_most(step):
        wait_slab(step)
        wait_spread(step, False)
        gradient(step, before_last, rows - 1)

    def gradient_last(step):
        wait_spread(step, True)
        gradient(step, last, 1)

    def run_step(step, part, origin, which=None):
        for cond, at, slot, onward, side, begun in (
            (row > 0, row + step, row + step + 1, run_right, part, col == origin),
            (row < rows - 1, row - step, row - step, run_left, 1 - part, col != origin),
        ):
            cond = both(which, both(begun, both(cond, jnp.logical_and(at >= 0, at < rows))))
            run_here(cond, slot, side)

            def add(at=at, slot=slot, side=side):
                add_running(at, slot, side)

            where(cond, add)
            onward(cond, at, side, ("run", step, part, origin, which is near))

    def wait_first():
        weight_here[1]()
        cot_here[1]()

    def wait_own(which):
        cond, wait = own_tokens[0 if which is near else 1]
        where(cond, wait)

    def inner_queries(part):
        side = owner if part == 0 else 1 - owner
        for step in reversed(range(1, rows)):
            on_sides(step, lambda at: query_part(at, side), inside)
        query_part(row, side)

    wait_first()
    parts_make(0)
    spread_step(0)
    for step in range(1, rows):
        tokens_in(step, near)
    wait_own(near)
    slabs_out(near, mine, at_slab)
    parts_out(0, far)
    for step in reversed(range(1, rows)):
        run_begin(0, near, step)
    cots_in(1)
    for step in range(1, rows):
        tokens_in(step, far)
        crossed(far, step)
        run_begin(0, far, step)
    wait_own(far)
    crossed(far, 0)
    slabs_out(far, mine, at_slab)
    slabs_out(far, theirs, at_pair)
    for step in reversed(range(1, rows)):
        run_begin(1, far, step, step < rows - 1)
    inner_queries(0)
    for step in reversed(range(2, rows)):
        run_step(step, 0, 0, near)
    parts_make(1)
    settled = len(pending)
    parts_out(1)
    slabs_across(near)
    cots_in(2)
    run_step(1, 0, 1, far)
    run_step(1, 0, 0, near)
    for step in reversed(range(rows)):
        crossed(near, step)
        if step:
            run_begin(1, near, step, step < rows - 1)
    slabs_out(near, theirs, at_pair)
    there = flip(depth, 1)
    across = pl.ds(pl.multiple_of(there * owned, owned), owned)
    go(None, line.at[:, :, across], slabs.at[0], at_slab + 1, depth_to=there)
    inner_queries(1)

    def near_depths():
        gradient(0)
        wait_whole(1)
        gradient(1)

    where(inside, near_depths)
    for step in range(2, rows):
        run_step(step, 0, 1, far)
    run_step(1, 0, 0, far)
    slabs_across(far)
    parts_make(2)
    parts_out(2)
    spread_step(1)
    for step in range(3, rows):
        cots_in(step)
        parts_make(step)
        parts_out(step)
    parts_out(0, near)
    where(at_end, near_depths)
    for step in range(2, rows - 1):
        spread_step(step)
    early_pieces = jnp.logical_or(near, at_end)
    pieces_home(1, early_pieces)
    for step in reversed(range(2, rows)):
        run_step(step, 1, 0)
        run_step(step, 1, 1)
    run_step(1, 0, 1, near)
    for step in range(2, depths):
        gradient_most(step)
    pieces_home(2, at_end)
    spread_step(rows - 1)
    for step in range(2, depths):
        gradient_last(step)

    slow = {index for key, index in shared.items() if key[0] == "begin1"}
    done = [entry for entry in pending[:settled] if entry[2] not in slow]
    pending[:settled] = [entry for entry in pending[:settled] if entry[2] in slow]
    for cond, wait, index in pooled + done:
        where(cond, wait)
        if index not in shared.values():
            spare.append(index)
    spare.extend({index for key, index in shared.items() if key[0] in ("tokens", "begin0")})
    for index, single in enumerate(singles):
        pl.semaphore_signal(
            ready_sem.at[index],
            inc=1,
            device_id=(row, col, flip(depth, single)),
            device_id_type=MESH,
        )
    for _, wait in moments:
        wait()

    send_rows = owned // SEND_PARTS

    def weight_rows(at, part):
        start = at * owned + part * send_rows
        return pl.ds(pl.multiple_of(start, send_rows), send_rows)

    def optimize(part):
        master_in(part).wait()

        def rows_of(index, carry):
            down = pl.ds(pl.multiple_of(index * 16, 16), 16)
            whole = pl.ds(pl.multiple_of(part * part_rows + index * 16, 16), 16)
            kept = pl.ds(pl.multiple_of(depth * owned + part * part_rows + index * 16, 16), 16)
            grad = product[whole] * grad_scale
            new_first = beta_one * first[whole] + (1.0 - beta_one) * grad
            new_second = beta_two * second[whole] + (1.0 - beta_two) * grad * grad
            step_value = new_first / bias_one / (jnp.sqrt(new_second / bias_two) + adam_eps)
            old = masters[part % 2, down]
            new_master = old - learn_rate * (step_value + decay_rate * old)
            product[whole] = new_master
            first[whole] = new_first
            second[whole] = new_second
            pool[kept] = new_master.astype(pool.dtype)
            return carry

        lax.fori_loop(0, part_rows // 16, rows_of, 0)
        if part + 2 < STATE_PARTS:
            master_in(part + 2).start()
        if (part + 1) % (STATE_PARTS // SEND_PARTS):
            return
        sent = part // (STATE_PARTS // SEND_PARTS)
        source = pool.at[weight_rows(depth, sent)]
        for index, single in reversed(list(enumerate(singles))):
            if sent == 0:
                pl.semaphore_wait(ready_sem.at[index], 1)
            go(
                None,
                source,
                source,
                at_weight + single * SEND_PARTS + sent,
                depth_to=flip(depth, single),
            )

    for part in range(STATE_PARTS):
        optimize(part)
    pieces_home(1, jnp.logical_not(early_pieces))
    pieces_home(2, inside)
    for step in range(3, rows):
        pieces_home(step)
    for step in reversed(range(1, rows - 1)):
        run_out(1, None, step)
    run_step(1, 1, 1, near)
    pieces_home(0)
    own_piece = load(near, piece.at[row], token_grad.at[:, columns_of(row, col)])
    go(
        far,
        piece.at[row],
        token_grad.at[:, columns_of(row, col)],
        at_final + row,
        col_to=other,
    )
    for step in range(1, rows):
        for at, cond in ((row - step, row >= step), (row + step, row + step < rows)):
            across = at // per_col != col
            arrived(both(cond, across), landed.at[at], at_piece + at)
            go(
                both(cond, across),
                landed.at[at],
                token_grad.at[:, columns_of(at, col)],
                at_final + at,
                col_to=other,
            )

    run_step(1, 1, 0, far)
    run_step(1, 1, 0, near)
    run_step(1, 1, 1, far)

    for sent in range(SEND_PARTS):
        for step in composites:
            have, low = relay_of(step)
            source = pool.at[weight_rows(flip(depth, have), sent)]
            if step - have == 1:
                arrived(None, source, at_weight + have * SEND_PARTS + sent)
            go(
                None,
                source,
                source,
                at_weight + step * SEND_PARTS + sent,
                depth_to=flip(depth, low),
            )

    from_left, from_right = row > 0, row < rows - 1
    for side in range(2):
        for cond, slot in ((from_left, row + 1), (from_right, row)):
            run_here(cond, slot, side)

            def add(slot=slot, side=side):
                add_running(row, slot, side)

            where(cond, add)

    def rounded(index, carry):
        down = pl.ds(pl.multiple_of(index * 16, 16), 16)
        query[down] = partial[row, down].astype(query.dtype)
        return carry

    lax.fori_loop(0, block // 16, rounded, 0)

    for at in range(rows):
        away = jnp.logical_and(at != row, at // per_col == col)
        arrived(away, token_grad.at[:, columns_of(at, col)], at_piece + at)
        arrived(at // per_col == col, token_grad.at[:, columns_of(at, other)], at_final + at)
    for sent in range(SEND_PARTS):
        for step in range(1, depths):
            if step not in stored:
                place = at_weight + step * SEND_PARTS + sent
                arrived(None, pool.at[weight_rows(flip(depth, step), sent)], place)
    counts.append((next(locals_), next(sends), next(places)))
    where(*own_piece)
    for cond, wait, _ in pending:
        where(cond, wait)


def write_out(*refs):
    held, outs, sem = refs[:6], refs[6:12], refs[12]
    copies = []
    for index, (source, target) in enumerate(zip(held, outs)):
        copies.append(
            pltpu.make_async_copy(
                source.at[pl.ds(0, target.shape[0])], target, sem.at[index]
            )
        )
    for copy in copies:
        copy.start()
    for copy in copies:
        copy.wait()


def step(mesh, tokens, weight, cotangent, master, first_moment, second_moment):
    rows, cols, depths = (mesh.shape[name] for name in ("row", "col", "depth"))
    block, width = tokens.shape[0], weight.shape[0]
    out_width, owned = weight.shape[1], master.shape[0]
    fits = (
        cols == 2
        and rows > 2
        and rows % 2 == 0
        and depths > 2
        and depths & (depths - 1) == 0
        and block % 32 == 0
        and width % 256 == 0
        and out_width % 128 == 0
        and owned % (16 * STATE_PARTS) == 0
    )
    small, wide = jnp.bfloat16, jnp.float32
    pool_rows = max(depths * rows * block, width)
    shapes = [
        ((width, out_width), small),
        ((block // 2, tokens.shape[1]), small),
        ((rows, block, width), small),
        ((depths - 1, rows, block, owned), small),
        ((owned, rows * block), small),
        ((rows, block, out_width), wide),
        ((rows + 1, block, out_width), wide),
        ((2, rows, block, width // 2), wide),
        ((rows, block, width // 2), wide),
        ((rows, block, width // 2), small),
        ((rows, block, width // 2), small),
        ((2, owned // STATE_PARTS, out_width), wide),
    ]
    total_tokens = block * rows * depths
    outs = [
        ((block, out_width), small),
        (tokens.shape, small),
        (master.shape, wide),
        (master.shape, wide),
        (master.shape, wide),
        ((pool_rows, out_width), small),
    ]
    held_bytes = sum(math.prod(shape) * jnp.dtype(dtype).itemsize for shape, dtype in shapes + outs)
    if not fits or held_bytes > VMEM_BYTES:
        return plain(tokens, weight, cotangent, master, first_moment, second_moment)

    def moved(counts, *semaphores):
        return pl.pallas_call(
            functools.partial(fused, rows, depths, 1.0 / math.sqrt(total_tokens), counts),
            out_shape=[pltpu.VMEM(shape, dtype) for shape, dtype in outs],
            in_specs=[pl.BlockSpec(memory_space=pl.ANY)] * 6,
            out_specs=[pl.BlockSpec(memory_space=pltpu.VMEM)] * 6,
            scratch_shapes=[pltpu.VMEM(shape, dtype) for shape, dtype in shapes]
            + [pltpu.SemaphoreType.DMA((count,)) for count in semaphores]
            + [pltpu.SemaphoreType.REGULAR((depths.bit_length() - 1,))],
            compiler_params=pltpu.CompilerParams(
                collective_id=0, has_side_effects=True, vmem_limit_bytes=VMEM_LIMIT
            ),
        )

    arrays = (tokens, weight, cotangent, master, first_moment, second_moment)
    counts = []
    jax.eval_shape(moved(counts, 512, 512, 512), *arrays)
    held = moved([], *counts[0])(*arrays)
    outs[-1] = (weight.shape, small)
    return pl.pallas_call(
        write_out,
        out_shape=[jax.ShapeDtypeStruct(shape, dtype) for shape, dtype in outs],
        in_specs=[pl.BlockSpec(memory_space=pltpu.VMEM)] * 6,
        out_specs=[pl.BlockSpec(memory_space=pl.ANY)] * 6,
        scratch_shapes=[pltpu.SemaphoreType.DMA((6,))],
        compiler_params=pltpu.CompilerParams(vmem_limit_bytes=1 << 20),
    )(*(pltpu.with_memory_space_constraint(value, pltpu.VMEM) for value in held))


def solution(mesh):
    in_specs = (
        P(("row", "depth"), "col"),
        P("row", "col"),
        P(("row", "depth"), "col"),
        P(("row", "depth"), "col"),
        P(("row", "depth"), "col"),
        P(("row", "depth"), "col"),
    )
    out_specs = (
        P(("row", "depth"), "col"),
        P(("row", "depth"), "col"),
        P(("row", "depth"), "col"),
        P(("row", "depth"), "col"),
        P(("row", "depth"), "col"),
        P("row", "col"),
    )
    return jax.shard_map(functools.partial(step, mesh), mesh=mesh, in_specs=in_specs, out_specs=out_specs, check_vma=False)
```
